32 devices in a mesh: dp: 8 (over y, x, core), tensor: 4 (over z).
Axes of the slice: x: 2, y: 2, z: 4, core: 2. Of those that a mesh axis runs over, the one named last changes fastest.
Arguments:
- tokens: bfloat16 [4096, 1152], P('dp'), may hold values from -6 to 6
- conditioning: bfloat16 [8, 4, 1152], P('dp'), may hold values from -6 to 6
- segments: int32 [8, 512], P('dp'), may hold values from 0 to 15, never falling along the last dimension, each value on 1 to 128 neighbouring positions
- crop_cond: int32 [8, 16], P('dp'), may hold values from 0 to 3
- w_ada: bfloat16 [1152, 6912], P(None, 'tensor'), may hold values from -0.1875 to 0.1875
- b_ada: bfloat16 [6912], P('tensor'), may hold values from -2 to 2
- w_qkv: bfloat16 [1152, 3, 1152], P(None, None, 'tensor'), may hold values from -0.25 to 0.25
- w_out: bfloat16 [1152, 1152], P(None, 'tensor'), may hold values from -0.5 to 0.5
- b_out: bfloat16 [1152], replicated, may hold values from -2 to 2
- w_up: bfloat16 [1152, 4608], P(None, 'tensor'), may hold values from -0.1875 to 0.1875
- b_up: bfloat16 [4608], P('tensor'), may hold values from -2 to 2
- w_down: bfloat16 [1152, 4608], P(None, 'tensor'), may hold values from -0.125 to 0.125
- b_down: bfloat16 [1152], replicated, may hold values from -2 to 2
- d_out: bfloat16 [4096, 1152], P('dp'), may hold values from -6 to 6
Outputs:
- output: bfloat16 [4096, 1152], P('dp')
- d_tokens: float32 [4096, 1152], P('dp')
- d_conditioning: float32 [8, 4, 1152], P('dp')
- d_w_ada: float32 [1152, 6912], P('dp', 'tensor')
- d_b_ada: float32 [6912], P('tensor')
- d_w_qkv: float32 [1152, 3, 1152], P('dp', None, 'tensor')
- d_w_out: float32 [1152, 1152], P('dp', 'tensor')
- d_b_out: float32 [1152], replicated
- d_w_up: float32 [1152, 4608], P('dp', 'tensor')
- d_b_up: float32 [4608], P('tensor')
- d_w_down: float32 [1152, 4608], P('dp', 'tensor')
- d_b_down: float32 [1152], replicated
The draws below stay inside these ranges and needn't reach their ends.
Inputs may be any that keep to these rules, and one draw needn't show every extreme that they name: `segments`: in each sequence the numbers never fall, every crop of 0 to 15 has 1 to 128 tokens, and one has exactly 128. `crop_cond`: each crop's number picks one of its own sequence's 4 conditioning vectors.
All inputs are finite; a program needn't handle non-finite values.
Results may differ from the reference program's by a relative error of at most 0.018.
Values may be sent and summed in bfloat16 or wider, within the bound.
No kernel may reach another device: no remote copies, remote signals or barrier semaphores. Data moves between devices by JAX's collectives and lax.ppermute only.
A program may use at most 128 MiB of HBM per device.

```python
import math
import jax
import jax.numpy as jnp
import numpy as np
from jax import lax

D = 1152
H = 16
HD = 72
FF = 4608
LEN = 512
CROPS = 16
CONDS = 4
SPAN = 128
SEQS = 8
TOKENS = 4096


def place_ends(values, own_key, least, high):
    index_at = [jax.random.randint(jax.random.fold_in(own_key, axis), (), 0, length) for axis, length in enumerate(values.shape)]
    main_axis = values.shape.index(max(values.shape))
    neighbour = index_at[:main_axis] + [(index_at[main_axis] + 1) % values.shape[main_axis]] + index_at[main_axis + 1:]
    return values.at[tuple(index_at)].set(least).at[tuple(neighbour)].set(high)


def spiked(entries, key, source, target, shards_of, factor):
    def block_of(position):
        return (jnp.arange(entries.shape[position]) // (entries.shape[position] // shards_of)).reshape((-1,) + (1,) * (entries.ndim - 1 - position))

    near = jax.random.permutation(key, shards_of)[block_of(target)]
    far = (block_of(target) + shards_of // 2) % shards_of
    return jnp.where((block_of(source) == near) | (block_of(source) == far), factor * entries, entries)


def block_scale(key, shape, cuts, smallest, high):
    factor_of, own = 1.0, jax.random.fold_in(key, 6)
    for dim, blocks in cuts:
        heights = jnp.exp(jax.random.uniform(jax.random.fold_in(own, dim), (blocks,), jnp.float32, smallest / len(cuts), high / len(cuts)))
        factor_of = factor_of * jnp.repeat(heights, shape[dim] // blocks).reshape([-1 if axis == dim else 1 for axis in range(len(shape))])
    return factor_of


def profile(number_of, total, bound, slope):
    weights = [(1 << 20) // math.isqrt(standing ** slope) + 1 for standing in range(2, number_of + 1)]
    rest, counts = total - bound - (number_of - 1), [1] * (number_of - 1)
    while rest > 0:
        candidates = [i for i in range(number_of - 1) if counts[i] < bound]
        pool, remaining = sum([weights[i] for i in candidates]), rest
        for i in candidates:
            more = min(bound - counts[i], max(1, remaining * weights[i] // pool), rest)
            counts[i] = counts[i] + more
            rest = rest - more
    return np.array([bound] + counts)


def uneven(key, count, total, limit, slope):
    if count == 2:
        one = jax.random.randint(key, (), max(1, total - limit), min(limit, total - 1) + 1)
        return jnp.stack([one, total - one])
    lengths = jnp.asarray(profile(count, total, limit, slope), jnp.int32)
    pairs = (count - 1) // 2
    source_of, taker = lengths[1:1 + 2 * pairs:2], lengths[2:2 + 2 * pairs:2]
    margin = jnp.minimum(source_of - 1, limit - taker)
    shifted = jax.random.randint(jax.random.fold_in(key, 1), (pairs,), 0, 1 << 20) % (margin + 1)
    lengths = lengths.at[1:1 + 2 * pairs:2].set(source_of - shifted).at[2:2 + 2 * pairs:2].set(taker + shifted)
    return lengths[jax.random.permutation(jax.random.fold_in(key, 2), count)]


def bell_draw(own_key, shape, scale, most, pieces=(), held_as=jnp.bfloat16):
    loudness = block_scale(own_key, shape, pieces, -0.22, 0.18) if pieces else 1.0
    array = jax.random.normal(own_key, shape, jnp.float32) * scale * loudness
    return jnp.minimum(jnp.maximum(array, -most), most).astype(held_as)


def bell_draw_with(own_key, extent, spread, reach, cuts, heavy, kind=jnp.bfloat16):
    drawn = spread * jax.random.normal(own_key, extent, jnp.float32)
    if cuts:
        drawn = drawn * block_scale(own_key, extent, cuts, -0.22, 0.18)
    return jnp.clip(spiked(drawn, jax.random.fold_in(own_key, 3), *heavy), -reach, reach).astype(kind)


def setup_inputs(seed: int = 0) -> dict:
    keys = jax.random.split(jax.random.key(seed), 15)
    tokens = bell_draw(keys[0], (TOKENS, D), 1.0, 6.0, ((0, 8),))
    conditioning = bell_draw(keys[1], (SEQS, CONDS, D), 1.0, 6.0, ((0, 8),))
    segments = jax.vmap(lambda own: jnp.searchsorted(jnp.cumsum(uneven(own, CROPS, LEN, SPAN, 1)), jnp.arange(LEN), side="right"))(jax.random.split(keys[2], SEQS)).reshape((SEQS, LEN)).astype(jnp.int32)
    crop_cond = place_ends(jax.random.randint(keys[3], (SEQS, CROPS), 0, CONDS), jax.random.fold_in(keys[3], 1), 0, CONDS - 1).astype(jnp.int32)
    w_ada = bell_draw(keys[4], (D, 6 * D), D ** -0.5, 0.1875, ((1, 4),))
    b_ada = bell_draw(keys[5], (6 * D,), 0.3, 2.0, ((0, 4),))
    w_qkv = bell_draw(keys[6], (D, 3, D), (D // 2) ** -0.5, 0.25, ((2, 4),))
    w_out = bell_draw(keys[7], (D, D), (D // 8) ** -0.5, 0.5, ((1, 4),))
    b_out = bell_draw(keys[8], (D,), 0.3, 2.0)
    w_up = bell_draw(keys[9], (D, FF), D ** -0.5, 0.1875, ((1, 4),))
    b_up = bell_draw(keys[10], (FF,), 0.3, 2.0, ((0, 4),))
    w_down = bell_draw(keys[11], (D, FF), (FF // 2) ** -0.5, 0.125, ((1, 4),))
    b_down = bell_draw(keys[12], (D,), 0.3, 2.0)
    d_out = bell_draw_with(keys[13], (TOKENS, D), 1.0, 6.0, ((0, 8),), (0, 1, 8, 2.0))
    return {"tokens": tokens, "conditioning": conditioning, "segments": segments, "crop_cond": crop_cond, "w_ada": w_ada, "b_ada": b_ada, "w_qkv": w_qkv, "w_out": w_out, "b_out": b_out, "w_up": w_up, "b_up": b_up, "w_down": w_down, "b_down": b_down, "d_out": d_out}


HIGHEST = lax.Precision.HIGHEST

@jax.custom_vjp
def low(v):
    return lax.optimization_barrier(v.astype(jnp.bfloat16)).astype(jnp.float32)

@jax.custom_vjp
def low_back(v):
    return v

def low_keep(v):
    return (low(v), None)

def low_pass(kept, grad):
    return (grad,)

def back_keep(v):
    return (v, None)

def back_low(kept, grad):
    return (low(grad),)
low.defvjp(low_keep, low_pass)
low_back.defvjp(back_keep, back_low)

def normalize(values):
    average = lax.optimization_barrier(jnp.mean(values, -1, keepdims=True))
    centered = values - average
    variance = lax.optimization_barrier(jnp.mean(centered * centered, -1, keepdims=True))
    return centered * lax.rsqrt(variance + 1e-06)

def attend_one(queries, key_vecs, values, segment_row):
    scores = jnp.einsum('qhd,khd->hqk', queries, key_vecs, precision=HIGHEST) * HD ** (-0.5)
    scores = low_back(scores)
    same_crop = segment_row[:, None] == segment_row[None, :]
    scores = jnp.where(same_crop[None], scores, -1e+30)
    largest = lax.optimization_barrier(jnp.max(scores, -1, keepdims=True))
    exponent = jnp.exp(scores - largest)
    soft_probs = exponent / lax.optimization_barrier(jnp.sum(exponent, -1, keepdims=True))
    low_probs = low(soft_probs)
    return jnp.einsum('hqk,khd->qhd', low_probs, values, precision=HIGHEST)

def forward(tokens, conditioning, w_ada, b_ada, w_qkv, w_out, b_out, w_up, b_up, w_down, b_down, segments, crop_cond):
    silu_cond = low(jax.nn.silu(conditioning))
    raw_mod = jnp.einsum('skd,de->ske', silu_cond, w_ada, precision=HIGHEST) + b_ada
    modulation = low(low_back(raw_mod))
    token_cond = jnp.take_along_axis(crop_cond, segments, axis=1)
    onehot = (token_cond[:, :, None] == jnp.arange(CONDS)[None, None, :]).astype(jnp.float32)
    per_token = jnp.einsum('stk,ske->ste', onehot, modulation, precision=HIGHEST).reshape(TOKENS, 6 * D)
    shift_attn, scale_attn, gate_attn, shift_mlp, scale_mlp, gate_mlp = jnp.split(per_token, 6, axis=1)
    first_in = low(normalize(tokens) * (1.0 + scale_attn) + shift_attn)
    projected = jnp.einsum('td,dje->tje', first_in, w_qkv, precision=HIGHEST)
    projected = low(low_back(projected))
    queries = projected[:, 0].reshape(SEQS, LEN, H, HD)
    key_vecs = projected[:, 1].reshape(SEQS, LEN, H, HD)
    values = projected[:, 2].reshape(SEQS, LEN, H, HD)
    checked = jax.checkpoint(attend_one)
    attended = lax.map(lambda packed: checked(*packed), (queries, key_vecs, values, segments))
    attended = low(low_back(attended.reshape(TOKENS, D)))
    branch = low_back(jnp.dot(attended, w_out.T, precision=HIGHEST) + b_out)
    middle = tokens + gate_attn * branch
    second_in = low(normalize(middle) * (1.0 + scale_mlp) + shift_mlp)
    pre_act = low_back(jnp.dot(second_in, w_up, precision=HIGHEST) + b_up)
    hidden = low(jax.nn.gelu(pre_act, approximate=True))
    mlp_out = low_back(jnp.dot(hidden, w_down.T, precision=HIGHEST) + b_down)
    return middle + gate_mlp * mlp_out

def reference(tokens, conditioning, segments, crop_cond, w_ada, b_ada, w_qkv, w_out, b_out, w_up, b_up, w_down, b_down, d_out):
    floats = tuple((array_in.astype(jnp.float32) for array_in in (tokens, conditioning, w_ada, b_ada, w_qkv, w_out, b_out, w_up, b_up, w_down, b_down)))

    def closed(*inputs):
        return forward(*inputs, segments, crop_cond)
    result, pullback = jax.vjp(closed, *floats)
    grads = pullback(d_out.astype(jnp.float32))
    return (result.astype(jnp.bfloat16), grads[0], grads[1], grads[2], grads[3], grads[4], grads[5], grads[6], grads[7], grads[8], grads[9], grads[10])
```

```python
import math
from functools import partial

import jax
import jax.numpy as jnp
from jax import lax
from jax.sharding import PartitionSpec as P

HD = 72
F32 = jnp.float32
LOW = jnp.bfloat16


def normalize_rows(values):
    average = jnp.mean(values, -1, keepdims=True)
    centered = values - average
    variance = jnp.mean(centered * centered, -1, keepdims=True)
    inverse = lax.rsqrt(variance + 1e-06)
    return (centered * inverse, inverse)


def normalize_back(gradient, normed, inverse):
    return inverse * (
        gradient
        - jnp.mean(gradient, -1, keepdims=True)
        - normed * jnp.mean(gradient * normed, -1, keepdims=True)
    )


def attend_forward(queries, key_vecs, values, segment_row, head_scale):
    scores = (
        jnp.einsum("qhd,khd->hqk", queries, key_vecs, preferred_element_type=F32) * head_scale
    )
    same_crop = (segment_row[:, None] == segment_row[None, :])[None]
    scores = jnp.where(same_crop, scores, -1e30)
    largest = jnp.max(scores, -1, keepdims=True)
    exponent = jnp.exp(scores - largest)
    denominator = jnp.sum(exponent, -1, keepdims=True)
    low_probs = (exponent / denominator).astype(LOW)
    attended = jnp.einsum("hqk,khd->qhd", low_probs, values, preferred_element_type=F32)
    return (attended.astype(LOW), largest + jnp.log(denominator))


def attend_backward(queries, key_vecs, values, segment_row, logsum, d_attended, head_scale):
    scores = (
        jnp.einsum("qhd,khd->hqk", queries, key_vecs, preferred_element_type=F32) * head_scale
    )
    same_crop = (segment_row[:, None] == segment_row[None, :])[None]
    soft_probs = jnp.where(same_crop, jnp.exp(scores - logsum), 0.0)
    low_probs = soft_probs.astype(LOW)
    d_values = jnp.einsum("hqk,qhd->khd", low_probs, d_attended, preferred_element_type=F32)
    d_probs = jnp.einsum("qhd,khd->hqk", d_attended, values, preferred_element_type=F32)
    d_scores = (soft_probs * (d_probs - jnp.sum(d_probs * soft_probs, -1, keepdims=True))).astype(
        LOW
    )
    d_queries = (
        jnp.einsum("hqk,khd->qhd", d_scores, key_vecs, preferred_element_type=F32) * head_scale
    )
    d_keys = (
        jnp.einsum("hqk,qhd->khd", d_scores, queries, preferred_element_type=F32) * head_scale
    )
    return (d_queries, d_keys, d_values)


def shards(
    tokens,
    conditioning,
    segments,
    crop_cond,
    w_ada,
    b_ada,
    w_qkv,
    w_out,
    b_out,
    w_up,
    b_up,
    w_down,
    b_down,
    d_out,
):
    tok_rows, width = tokens.shape
    seq_count, seq_length = segments.shape
    cond_count = conditioning.shape[1]
    crop_count = crop_cond.shape[1]
    local_width = w_qkv.shape[2]
    head_count = local_width // HD
    head_scale = HD ** (-0.5)
    parts = lax.axis_size("tensor")
    dp_count = lax.axis_size("dp")
    me = lax.axis_index("tensor")
    dp_me = lax.axis_index("dp")
    share = seq_length // parts

    def rotate(values_in):
        return jnp.roll(values_in, -me * share, 1)

    def from_ahead(value, step):
        return lax.ppermute(value, "tensor", [(s, (s - step) % parts) for s in range(parts)])

    def to_ahead(value, step):
        return lax.ppermute(value, "tensor", [(s, (s + step) % parts) for s in range(parts)])

    steps = sorted(range(1, parts), key=lambda k: (-min(k, parts - k), k))

    def gather_blocks(own):
        blocks = [own] + [None] * (parts - 1)
        for k in steps:
            blocks[k] = from_ahead(own, k)
        return blocks

    def scatter_blocks(make):
        arrived = [to_ahead(make(k).astype(LOW), k) for k in steps]
        total = make(0)
        for one in arrived:
            total = total + one.astype(F32)
        return total

    def join(blocks):
        each = [b.reshape(seq_count, share, b.shape[-1]) for b in blocks]
        return jnp.concatenate(each, 1).reshape(tok_rows, blocks[0].shape[-1])

    def block(values_in, k):
        cube = values_in.reshape(seq_count, seq_length, values_in.shape[-1])
        return cube[:, k * share : (k + 1) * share].reshape(seq_count * share, -1)

    def unrotate(blocks):
        cube = join(blocks).reshape(seq_count, seq_length, -1)
        return jnp.roll(cube, me * share, 1).reshape(tok_rows, -1)

    levels = []
    left = dp_count
    stride = 1
    while left > 1:
        radix = 2 if (left % 4 or left == dp_count) and left % 2 == 0 else 4
        levels.append((stride, radix))
        stride *= radix
        left //= radix

    def dp_swap(value, distance):
        return lax.ppermute(value, "dp", [(s, s ^ distance) for s in range(dp_count)])

    def dp_scatter(grads):
        rows, columns = grads.shape[1:]
        current = grads
        remaining = dp_count
        for stride, radix in levels:
            digit = (dp_me // stride) % radix
            remaining //= radix
            view = current.reshape(remaining, radix, rows, columns)
            total = lax.dynamic_index_in_dim(view, digit, 1, False).astype(F32)
            for m in sorted(range(1, radix), reverse=True):
                piece = lax.dynamic_index_in_dim(view, digit ^ m, 1, False).astype(LOW)
                total = total + dp_swap(piece, m * stride).astype(F32)
            current = total
        return current.reshape(rows, columns)

    tokens = rotate(tokens.reshape(seq_count, seq_length, width)).reshape(tok_rows, width)
    d_out = rotate(d_out.reshape(seq_count, seq_length, width)).reshape(tok_rows, width)
    segments = rotate(segments)

    cond_act, silu_back = jax.vjp(jax.nn.silu, conditioning.astype(F32))
    cond_low = cond_act.astype(LOW).reshape(seq_count * cond_count, width)
    mod_part = (
        jnp.dot(cond_low, w_ada, preferred_element_type=F32) + b_ada.astype(F32)
    ).astype(LOW)
    mod_blocks = jnp.stack(gather_blocks(mod_part))
    modulation = (
        jnp.roll(mod_blocks, me, 0).transpose(1, 0, 2).reshape(seq_count, cond_count, 6 * width)
    )
    crop_match = segments[:, :, None] == jnp.arange(crop_count, dtype=jnp.int32)[None, None, :]
    token_cond = jnp.sum(jnp.where(crop_match, crop_cond[:, None, :], 0), -1)
    onehot = (
        token_cond[:, :, None] == jnp.arange(cond_count, dtype=jnp.int32)[None, None, :]
    ).astype(LOW)

    def per_token(index, hot):
        return jnp.einsum(
            "stk,ske->ste",
            hot,
            modulation[:, :, index * width : (index + 1) * width],
            preferred_element_type=F32,
        ).reshape(-1, width)

    own_hot = onehot[:, :share]
    resid_in = tokens.astype(F32)
    normed_attn, inverse_attn = normalize_rows(resid_in)
    scale_attn = per_token(1, onehot)
    first_in = (normed_attn * (1.0 + scale_attn) + per_token(0, onehot)).astype(LOW)
    projected = jnp.einsum("td,dje->tje", first_in, w_qkv, preferred_element_type=F32).astype(LOW)
    qkv_heads = projected.reshape(seq_count, seq_length, 3, head_count, HD)
    queries = qkv_heads[:, :, 0]
    key_vecs = qkv_heads[:, :, 1]
    values = qkv_heads[:, :, 2]
    fwd = [
        attend_forward(queries[s], key_vecs[s], values[s], segments[s], head_scale)
        for s in range(seq_count)
    ]
    attended = jnp.stack([a for a, _ in fwd]).reshape(tok_rows, local_width)

    branch = scatter_blocks(
        lambda k: jnp.einsum(
            "te,de->td", block(attended, k), w_out, preferred_element_type=F32
        )
    ) + b_out.astype(F32)
    gradient = d_out.astype(F32)
    gradient_rows = block(gradient, 0)
    gate_attn_rows = per_token(2, own_hot)
    scale_mlp_rows = per_token(4, own_hot)
    middle = block(resid_in, 0) + gate_attn_rows * branch
    normed_mlp, inverse_mlp = normalize_rows(middle)
    second_rows = (normed_mlp * (1.0 + scale_mlp_rows) + per_token(3, own_hot)).astype(LOW)
    gate_mlp = per_token(5, onehot)
    d_mixed = (gradient * gate_mlp).astype(LOW)
    d_b_down = jnp.sum(d_mixed.astype(F32), 0)

    second_in = join(gather_blocks(second_rows))
    pre_act = jnp.dot(second_in, w_up, preferred_element_type=F32) + b_up.astype(F32)
    activated, gelu_back = jax.vjp(partial(jax.nn.gelu, approximate=True), pre_act)
    hidden = activated.astype(LOW)
    d_hidden = jnp.dot(d_mixed, w_down, preferred_element_type=F32)
    d_pre = gelu_back(d_hidden)[0].astype(LOW)
    d_second = scatter_blocks(
        lambda k: jnp.einsum("tf,df->td", block(d_pre, k), w_up, preferred_element_type=F32)
    )
    d_middle = gradient_rows + normalize_back(
        d_second * (1.0 + scale_mlp_rows), normed_mlp, inverse_mlp
    )
    branch_rows = (d_middle * gate_attn_rows).astype(LOW)
    d_gate_attn = d_middle * branch
    d_branch = join(gather_blocks(branch_rows))

    mlp_out = scatter_blocks(
        lambda k: jnp.einsum("tf,df->td", block(hidden, k), w_down, preferred_element_type=F32)
    ) + b_down.astype(F32)
    output_part = (middle + block(gate_mlp, 0) * mlp_out).astype(LOW)
    output = unrotate(gather_blocks(output_part))
    d_gate_mlp = gradient_rows * mlp_out

    def split(grad):
        return grad.reshape(dp_count, width // dp_count, -1)

    d_w_down = dp_scatter(
        split(jnp.einsum("td,tf->df", d_mixed, hidden, preferred_element_type=F32))
    )
    d_w_up = dp_scatter(
        split(jnp.einsum("td,tf->df", second_in, d_pre, preferred_element_type=F32))
    )
    d_b_up = jnp.sum(d_pre.astype(F32), 0)
    d_w_out = dp_scatter(
        split(jnp.einsum("td,te->de", d_branch, attended, preferred_element_type=F32))
    )
    d_b_out = jnp.sum(d_branch.astype(F32), 0)
    d_attended = jnp.dot(d_branch, w_out, preferred_element_type=F32).astype(LOW)
    d_attended = d_attended.reshape(seq_count, seq_length, head_count, HD)
    bwd = [
        attend_backward(
            queries[s], key_vecs[s], values[s], segments[s], fwd[s][1], d_attended[s], head_scale
        )
        for s in range(seq_count)
    ]
    d_projected = (
        jnp.stack([jnp.stack(b, 1) for b in bwd]).reshape(tok_rows, 3, local_width).astype(LOW)
    )
    d_first = scatter_blocks(
        lambda k: jnp.einsum(
            "tje,dje->td",
            block(d_projected.reshape(tok_rows, -1), k).reshape(-1, 3, local_width),
            w_qkv,
            preferred_element_type=F32,
        )
    )
    d_w_qkv = dp_scatter(
        split(jnp.einsum("td,tje->dje", first_in, d_projected, preferred_element_type=F32))
    ).reshape(width // dp_count, 3, local_width)
    normed_rows = block(normed_attn, 0)
    token_rows = d_middle + normalize_back(
        d_first * (1.0 + block(scale_attn, 0)), normed_rows, block(inverse_attn, 0)
    )
    d_tokens = unrotate(gather_blocks(token_rows.astype(LOW))).astype(F32)

    d_per_token = jnp.stack(
        (d_first, d_first * normed_rows, d_gate_attn, d_second, d_second * normed_mlp, d_gate_mlp)
    ).reshape(6, seq_count, share, width)
    mod_sums = jnp.einsum(
        "stk,jste->skje", own_hot.astype(F32), d_per_token, precision=lax.Precision.HIGHEST
    ).reshape(seq_count * cond_count, parts, -1)
    mod_turned = jnp.roll(mod_sums.transpose(1, 0, 2), -me, 0)
    d_mod_part = scatter_blocks(lambda k: mod_turned[k]).astype(LOW)
    d_silu_part = jnp.einsum("ke,de->kd", d_mod_part, w_ada, preferred_element_type=F32)
    d_silu_all = jnp.roll(jnp.stack(gather_blocks(d_silu_part)), me, 0)
    d_silu = jnp.sum(d_silu_all, 0)
    d_conditioning = silu_back(d_silu.reshape(seq_count, cond_count, width))[0]

    columns = width // dp_count
    cond_all = lax.all_gather(cond_low, "dp", axis=0, tiled=True)
    d_mod_all = lax.all_gather(d_mod_part, "dp", axis=0, tiled=True)
    cond_mine = lax.dynamic_slice_in_dim(cond_all, dp_me * columns, columns, 1)
    d_w_ada = jnp.einsum("kd,ke->de", cond_mine, d_mod_all, preferred_element_type=F32)
    d_b_ada = jnp.sum(d_mod_all.astype(F32), 0)
    d_b_out, d_b_up, d_b_down = lax.psum((d_b_out, d_b_up, d_b_down), "dp")
    return (
        output,
        d_tokens,
        d_conditioning,
        d_w_ada,
        d_b_ada,
        d_w_qkv,
        d_w_out,
        d_b_out,
        d_w_up,
        d_b_up,
        d_w_down,
        d_b_down,
    )


def solution(mesh):
    return jax.shard_map(
        shards,
        mesh=mesh,
        in_specs=(
            P("dp", None),
            P("dp", None, None),
            P("dp", None),
            P("dp", None),
            P(None, "tensor"),
            P("tensor"),
            P(None, None, "tensor"),
            P(None, "tensor"),
            P(),
            P(None, "tensor"),
            P("tensor"),
            P(None, "tensor"),
            P(),
            P("dp", None),
        ),
        out_specs=(
            P("dp", None),
            P("dp", None),
            P("dp", None, None),
            P("dp", "tensor"),
            P("tensor"),
            P("dp", None, "tensor"),
            P("dp", "tensor"),
            P(),
            P("dp", "tensor"),
            P("tensor"),
            P("dp", "tensor"),
            P(),
        ),
        check_vma=False,
    )
```

```python
import jax
import jax.numpy as jnp
from jax import lax
from jax.experimental import pallas as pl
from jax.experimental.pallas import tpu as pltpu
from jax.sharding import PartitionSpec as P

HD = 72
F32 = jnp.float32
LOW = jnp.bfloat16
NEG = -1e30
LOG2E = 1.4426950408889634
PIECES = 8
HOT = 8
HIGHEST = lax.Precision.HIGHEST
SMEM = pl.BlockSpec(memory_space=pltpu.SMEM)
HBM = pl.BlockSpec(memory_space=pltpu.HBM)
SMALL = pl.CostEstimate(flops=1 << 20, transcendentals=0, bytes_accessed=1 << 20)


def dot_nn(a, b):
    return lax.dot_general(a, b, (((1,), (0,)), ((), ())), preferred_element_type=F32)


def dot_nt(a, b):
    return lax.dot_general(a, b, (((1,), (1,)), ((), ())), preferred_element_type=F32)


def dot_tn(a, b):
    return lax.dot_general(a, b, (((0,), (0,)), ((), ())), preferred_element_type=F32)


def normalize_rows(values):
    average = jnp.mean(values, -1, keepdims=True)
    centered = values - average
    variance = jnp.mean(centered * centered, -1, keepdims=True)
    inverse = lax.rsqrt(variance + 1e-06)
    return (centered * inverse, inverse)


def normalize_back(gradient, normed, inverse):
    return inverse * (
        gradient
        - jnp.mean(gradient, -1, keepdims=True)
        - normed * jnp.mean(gradient * normed, -1, keepdims=True)
    )


def softmax_rows(queries, key_vecs, bias):
    scaled = dot_nt(queries, key_vecs) * (HD**-0.5 * LOG2E) + bias
    exponent = jnp.exp2(scaled - jnp.max(scaled, -1, keepdims=True))
    return exponent * (1.0 / jnp.sum(exponent, -1, keepdims=True))


def piece_copies(table, pair, into, sems):
    first, second, step, rows = pair
    ahead = first.shape[0]
    copies = []
    for n in range(PIECES):
        source = first.at[n] if n < ahead else second.at[n - ahead]
        source = source.at[step * rows : (step + 1) * rows, :]
        place = pl.ds(pl.multiple_of(table[n] * rows, 16), rows)
        copies.append(pltpu.make_async_copy(source, into.at[place, :], sems.at[n]))
    return copies


class Staged:
    def __init__(self, sources, ins, in_sems, outs, targets, out_sems):
        self.coming = [
            pltpu.make_async_copy(a, b, in_sems.at[n])
            for n, (a, b) in enumerate(zip(sources, ins))
        ]
        self.going = [
            pltpu.make_async_copy(a, b, out_sems.at[n])
            for n, (a, b) in enumerate(zip(outs, targets))
        ]
        self.ins, self.outs = ins, outs
        self.here, self.left = set(), set()
        for one in self.coming:
            one.start()

    def get(self, n):
        if n not in self.here:
            self.here.add(n)
            self.coming[n].wait()
        return self.ins[n]

    def put(self, n):
        self.left.add(n)
        self.going[n].start()

    def finish(self):
        for n in range(len(self.coming)):
            self.get(n)
        for n, one in enumerate(self.going):
            if n not in self.left:
                one.start()
        for one in self.going:
            one.wait()


OWN_ROWS = "rows"
OWN_COLUMNS = "columns"


def staged_call(body, scalars, ins, outs, name, mib, raw=(), scratch=(), small=True, share=0):
    plain = [one if isinstance(one, tuple) else (one, None) for one in ins]
    arrays = [one for one, _ in plain]
    shapes = []
    for one, kind in plain:
        shape = list(one.shape)
        if kind == OWN_ROWS:
            shape[0] = share
        if kind == OWN_COLUMNS:
            shape[1] = share
        shapes.append(pltpu.VMEM(tuple(shape), one.dtype))
    counts = [len(scalars), len(ins), len(raw), len(outs), len(ins), len(outs)]

    def kernel(*refs):
        groups, at = [], 0
        for count in counts:
            groups.append(refs[at : at + count])
            at += count
        scalar_refs, sources, raw_refs, targets, in_refs, out_refs = groups
        in_sems, out_sems = refs[at : at + 2]
        picked = []
        for source, (_, kind) in zip(sources, plain):
            if kind == OWN_ROWS:
                source = source.at[pl.ds(pl.multiple_of(scalar_refs[0][0] * share, 16), share), :]
            if kind == OWN_COLUMNS:
                source = source.at[:, pl.ds(pl.multiple_of(scalar_refs[0][0] * share, 128), share)]
            picked.append(source)
        staged = Staged(picked, in_refs, in_sems, out_refs, targets, out_sems)
        body(scalar_refs, staged, raw_refs, refs[at + 2 :])
        staged.finish()

    return pl.pallas_call(
        kernel,
        out_shape=tuple(outs),
        in_specs=[SMEM] * len(scalars) + [HBM] * (len(ins) + len(raw)),
        out_specs=(HBM,) * len(outs),
        scratch_shapes=shapes
        + [pltpu.VMEM(one.shape, one.dtype) for one in outs]
        + [pltpu.SemaphoreType.DMA((len(ins),)), pltpu.SemaphoreType.DMA((len(outs),))]
        + list(scratch),
        compiler_params=pltpu.CompilerParams(vmem_limit_bytes=mib << 20),
        cost_estimate=SMALL if small else None,
        name=name,
    )(*scalars, *arrays, *raw)


def shaped(shape, dtype):
    return jax.ShapeDtypeStruct(shape, dtype)


def modulate(hot, modulation, index):
    model = modulation.shape[1] // 6
    return dot_nn(hot[...], modulation[:, index * model : (index + 1) * model])


def fill_bias(bias, seg_col, seg_row):
    bias[...] = jnp.where(seg_col[...] == seg_row[...], 0.0, NEG)


def attend_group(table, first_in, seg_col, seg_row, pair, width):
    length, model = first_in.shape
    total = 4 * width

    def body(scalars, staged, raw, scratch):
        weights, bias, sems = scratch
        pieces = piece_copies(scalars[0], (*raw, pair[2], total // PIECES), weights, sems)
        for c in pieces:
            c.start()
        fill_bias(bias, staged.get(1), staged.get(2))
        projected, attended, w_out = staged.outs
        for c in pieces:
            c.wait()
        projected[...] = dot_nt(staged.get(0)[...], weights[: 3 * width]).astype(LOW)
        staged.put(0)
        w_out[...] = weights[3 * width :]
        staged.put(2)
        for h in range(width // HD):
            queries, key_vecs, values = [
                projected[:, j * width + h * HD : j * width + (h + 1) * HD] for j in range(3)
            ]
            probs = softmax_rows(queries, key_vecs, bias[...])
            attended[:, h * HD : (h + 1) * HD] = dot_nn(probs.astype(LOW), values).astype(LOW)

    return staged_call(
        body,
        [table],
        [first_in, seg_col, seg_row],
        [
            shaped((length, 3 * width), LOW),
            shaped((length, width), LOW),
            shaped((width, model), LOW),
        ],
        "attend_group",
        32,
        raw=pair[:2],
        scratch=[
            pltpu.VMEM((total, model), LOW),
            pltpu.VMEM((length, length), F32),
            pltpu.SemaphoreType.DMA((PIECES,)),
        ],
    )


def head_gradients(qkv, d_attended, bias, low_probs, d_scores, d_projected):
    width = d_attended.shape[1]
    scale = HD**-0.5
    for h in range(width // HD):
        columns = slice(h * HD, (h + 1) * HD)
        queries, key_vecs, values = [
            qkv[:, j * width + h * HD : j * width + (h + 1) * HD] for j in range(3)
        ]
        d_head = d_attended[:, columns]
        probs = softmax_rows(queries, key_vecs, bias[...])
        d_probs = dot_nt(d_head, values)
        inner = jnp.sum(d_probs * probs, -1, keepdims=True)
        low_probs[h] = probs.astype(LOW)
        d_scores[h] = (probs * (d_probs - inner)).astype(LOW)
        d_projected[:, h * HD : (h + 1) * HD] = (dot_nn(d_scores[h], key_vecs) * scale).astype(
            LOW
        )
        d_projected[:, width + h * HD : width + (h + 1) * HD] = (
            dot_tn(d_scores[h], queries) * scale
        ).astype(LOW)
        d_projected[:, 2 * width + h * HD : 2 * width + (h + 1) * HD] = dot_tn(
            low_probs[h], d_head
        ).astype(LOW)


def split_sum(hot_rows, values_in):
    high = values_in.astype(LOW)
    rest = values_in - high.astype(F32)
    mid = rest.astype(LOW)
    low = (rest - mid.astype(F32)).astype(LOW)
    return dot_nn(hot_rows, high) + dot_nn(hot_rows, mid) + dot_nn(hot_rows, low)


def mlp_forward(me, attended, w_out, b_out, tokens, hot, modulation, d_hidden, w_up, b_up):
    parts = len(attended)
    length, model = tokens.shape
    units = w_up.shape[1]
    share = length // parts

    def body(scalars, staged, raw, scratch):
        held = scratch[0]
        own_branch, own_middle, second_in, hidden, d_pre, d_second, d_b_up = staged.outs
        rows = length // 2
        sums = jnp.zeros((1, units), F32)
        for step in range(2):
            block = slice(step * rows, (step + 1) * rows)
            branch = staged.get(2 * parts)[...]
            for k in range(parts):
                branch = branch + dot_nn(staged.get(k)[block], staged.get(parts + k)[...])
            chosen, table = staged.get(2 * parts + 2)[block], staged.get(2 * parts + 3)
            stream = staged.get(2 * parts + 1)[block].astype(F32) + (
                modulate(chosen, table, 2) * branch
            )
            held[0, block] = branch
            held[1, block] = stream
            normed, _ = normalize_rows(stream)
            second = (normed * (1.0 + modulate(chosen, table, 4)) + modulate(chosen, table, 3)).astype(LOW)
            second_in[block] = second
            weights = staged.get(2 * parts + 5)
            u = dot_nn(second, weights[...]) + staged.get(2 * parts + 6)[...]
            root = 0.7978845608028654
            square = u * u
            bent = jnp.tanh(root * u * (1.0 + 0.044715 * square))
            half = 0.5 * (1.0 + bent)
            hidden[block] = (u * half).astype(LOW)
            slope = half + 0.5 * u * (1.0 - bent * bent) * (root * (1.0 + 3 * 0.044715 * square))
            low = (staged.get(2 * parts + 4)[block] * slope).astype(LOW)
            d_pre[block] = low
            sums = sums + jnp.sum(low.astype(F32), 0, keepdims=True)
            added = dot_nt(low, weights[...]).astype(LOW)
            for n in range(rows // share):
                d_second[step * (rows // share) + n] = added[n * share : (n + 1) * share]
        d_b_up[...] = sums
        mine = pl.ds(pl.multiple_of(scalars[0][0] * share, 8), share)
        own_branch[...] = held[0, mine, :]
        own_middle[...] = held[1, mine, :]

    return staged_call(
        body,
        [me],
        [*attended, *w_out, b_out, tokens, hot, modulation, d_hidden, w_up, b_up],
        [
            shaped((share, model), F32),
            shaped((share, model), F32),
            shaped((length, model), LOW),
            shaped((length, units), LOW),
            shaped((length, units), LOW),
            shaped((parts, share, model), LOW),
            shaped((1, units), F32),
        ],
        "mlp_forward",
        48,
        scratch=[pltpu.VMEM((2, length, model), F32)],
        small=False,
    )


def mlp_down(hidden, w_down, d_out, hot_rows, parts):
    length, model = d_out.shape
    share = length // parts
    count = hot_rows.shape[0]

    def body(scalars, staged, raw, scratch):
        low, sums = staged.outs
        total = jnp.zeros((count, model), F32)
        rows = length // 2
        for step in range(2):
            block = slice(step * rows, (step + 1) * rows)
            added = dot_nt(staged.get(0)[block], staged.get(1)[...])
            for n in range(rows // share):
                low[step * (rows // share) + n] = added[n * share : (n + 1) * share].astype(LOW)
            total = total + split_sum(
                staged.get(3)[:, block], staged.get(2)[block].astype(F32) * added
            )
        sums[...] = total

    return staged_call(
        body,
        [],
        [hidden, w_down, d_out, hot_rows],
        [shaped((parts, share, model), LOW), shaped((count, model), F32)],
        "mlp_down",
        32,
    )


def hand_out_types(halves, rows, columns):
    if halves is None:
        return [shaped((rows, columns), F32)]
    count, high = halves
    return [shaped((count, high, columns), F32), shaped((count, high, columns), LOW)]


def hand_out(digit, whole, outs):
    if len(outs) == 1:
        outs[0][...] = whole[...]
        return
    keep, send = outs
    count, high = keep.shape[:2]
    for n in range(count):
        keep[n] = whole[pl.ds(pl.multiple_of((2 * n + digit) * high, 8), high), :]
        send[n] = whole[pl.ds(pl.multiple_of((2 * n + 1 - digit) * high, 8), high), :].astype(LOW)


def mlp_grads(digit, d_mixed, hidden, second_in, d_pre, halves):
    model, units = d_mixed.shape[1], hidden.shape[1]

    def body(scalars, staged, raw, scratch):
        whole = scratch[0]
        whole[:, :units] = dot_tn(staged.get(0)[...], staged.get(1)[...])
        whole[:, units:] = dot_tn(staged.get(2)[...], staged.get(3)[...])
        hand_out(scalars[0][0], whole, staged.outs)

    return staged_call(
        body,
        [digit],
        [d_mixed, hidden, second_in, d_pre],
        hand_out_types(halves, model, 2 * units),
        "mlp_grads",
        48,
        scratch=[pltpu.VMEM((model, 2 * units), F32)],
    )


def level_sum(digit, keep, got):
    radix, rows, columns = keep.shape

    def body(scalars, staged, raw, scratch):
        mine = scalars[0][0]
        kept, came = staged.get(0), staged.get(1)
        for m in range(1, radix):
            other = jnp.bitwise_xor(mine, m)
            staged.outs[m][...] = (kept[other] + came[other].astype(F32)).astype(LOW)
            staged.put(m)
        staged.outs[0][...] = kept[mine] + came[mine].astype(F32)

    return staged_call(
        body,
        [digit],
        [keep, got],
        [shaped((rows, columns), F32)] + [shaped((rows, columns), LOW)] * (radix - 1),
        "level_sum",
        32,
    )


def finish_sum(own, got, types):
    def body(scalars, staged, raw, scratch):
        total = staged.get(0)[...]
        for n in range(len(got)):
            total = total + staged.get(n + 1)[...].astype(F32)
        at = 0
        for out in staged.outs:
            width = out.shape[-1]
            for j in range(out.shape[0] if len(out.shape) == 3 else 1):
                target = out.at[j] if len(out.shape) == 3 else out
                target[...] = total[:, at : at + width]
                at += width

    return staged_call(body, [], [own, *got], types, "finish_sum", 24)


def turn_back(me, arrived, modulation, middle, d_out, hot):
    parts, share, model = arrived.shape

    def body(scalars, staged, raw, scratch):
        spread, d_second, d_middle = staged.outs
        normed, inverse = normalize_rows(staged.get(2)[...])
        scale = modulate(staged.get(4), staged.get(1), 4)
        came = staged.get(0)
        grad = came[0].astype(F32)
        for k in range(1, parts):
            grad = grad + came[k].astype(F32)
        d_second[...] = grad
        moved = staged.get(3)[...].astype(F32) + normalize_back(
            grad * (1.0 + scale), normed, inverse
        )
        d_middle[...] = moved
        for k in range(parts):
            spread[k] = moved.astype(LOW)

    return staged_call(
        body,
        [me],
        [arrived, modulation, middle, (d_out, OWN_ROWS), (hot, OWN_ROWS)],
        [
            shaped(arrived.shape, LOW),
            shaped((share, model), F32),
            shaped((share, model), F32),
        ],
        "turn_back",
        16,
        share=share,
    )


def own_sums(me, branch, middle, d_second, d_middle, d_out, b_down, hot_rows, gate_sums):
    share, model = middle.shape
    count = hot_rows.shape[0]

    def body(scalars, staged, raw, scratch):
        sums = staged.outs[0]
        normed, _ = normalize_rows(staged.get(1)[...])
        second, moved = staged.get(2), staged.get(3)
        each = [
            moved[...] * staged.get(0)[...],
            second[...],
            second[...] * normed,
            staged.get(4)[...].astype(F32) * staged.get(5)[...],
        ]
        for n, one in enumerate(each):
            added = split_sum(staged.get(6)[...], one)
            if n == len(each) - 1:
                added = added + staged.get(7)[...]
            sums[:, n * model : (n + 1) * model] = added

    return staged_call(
        body,
        [me],
        [
            branch,
            middle,
            d_second,
            d_middle,
            (d_out, OWN_ROWS),
            b_down,
            (hot_rows, OWN_COLUMNS),
            gate_sums,
        ],
        [shaped((count, 4 * model), F32)],
        "own_sums",
        16,
        share=share,
    )[0]


def output_rows(me, arrived, b_down, middle, modulation, hot):
    parts, share, model = arrived.shape

    def body(scalars, staged, raw, scratch):
        came = staged.get(0)
        total = staged.get(1)[...]
        for k in range(parts):
            total = total + came[k].astype(F32)
        made = staged.get(2)[...] + modulate(staged.get(4), staged.get(3), 5) * total
        for k in range(parts):
            staged.outs[0][k] = made.astype(LOW)

    return staged_call(
        body,
        [me],
        [arrived, b_down, middle, modulation, (hot, OWN_ROWS)],
        [shaped(arrived.shape, LOW)],
        "output_rows",
        16,
        share=share,
    )[0]


def back_scratch(length, width):
    heads = width // HD
    return [
        pltpu.VMEM((length, width), LOW),
        pltpu.VMEM((heads, length, length), LOW),
        pltpu.VMEM((heads, length, length), LOW),
        pltpu.VMEM((length, length), F32),
    ]


def back_first(
    digit,
    d_middle,
    hot,
    modulation,
    seg_col,
    seg_row,
    w_out,
    qkv,
    first_in,
    attended,
    near_out,
    near_qkv,
    halves,
):
    length, model = d_middle.shape
    width = attended.shape[1]

    def body(scalars, staged, raw, scratch):
        d_attended, low_probs, d_scores, bias, whole = scratch
        d_branch, d_local, d_near, *outs, d_b_out = staged.outs
        gate = modulate(staged.get(1), staged.get(2), 2)
        d_branch[...] = (staged.get(0)[...].astype(F32) * gate).astype(LOW)
        staged.put(0)
        d_b_out[...] = jnp.sum(d_branch[...].astype(F32), 0, keepdims=True)
        fill_bias(bias, staged.get(3), staged.get(4))
        d_attended[...] = dot_nt(d_branch[...], staged.get(5)[...]).astype(LOW)
        head_gradients(staged.get(6), d_attended, bias, low_probs, d_scores, d_local)
        staged.put(1)
        whole[:, : 3 * width] = dot_tn(staged.get(7)[...], d_local[...])
        whole[:, 3 * width :] = dot_tn(d_branch[...], staged.get(8)[...])
        hand_out(scalars[0][0], whole, outs)
        for n in range(len(outs)):
            staged.put(3 + n)
        d_attended[...] = dot_nt(d_branch[...], staged.get(9)[...]).astype(LOW)
        head_gradients(staged.get(10), d_attended, bias, low_probs, d_scores, d_near)

    return staged_call(
        body,
        [digit],
        [
            d_middle,
            hot,
            modulation,
            seg_col,
            seg_row,
            w_out,
            qkv,
            first_in,
            attended,
            near_out,
            near_qkv,
        ],
        [
            shaped((length, model), LOW),
            shaped((length, 3 * width), LOW),
            shaped((length, 3 * width), LOW),
            *hand_out_types(halves, model, 4 * width),
            shaped((1, model), F32),
        ],
        "back_first",
        52,
        scratch=back_scratch(length, width) + [pltpu.VMEM((model, 4 * width), F32)],
    )


def back_remote(
    me,
    table,
    d_branch,
    seg_col,
    seg_row,
    d_local,
    d_near,
    w_qkv,
    hot,
    hot_rows,
    modulation,
    tokens,
    d_middle,
    pairs,
    saved,
):
    length, model = d_branch.shape
    width = d_local.shape[1] // 3
    remote = len(saved)
    parts = remote + 1
    rows = 4 * width // PIECES

    def body(scalars, staged, raw, scratch):
        (
            d_attended,
            low_probs,
            d_scores,
            bias,
            weights,
            projected,
            d_projected,
            d_first,
            sems,
            saved_sems,
        ) = scratch
        me_ref, table_ref = scalars
        pieces, qkvs = raw[: 2 * remote], raw[2 * remote :]
        d_tokens, sums = staged.outs

        def copies(k, slot):
            pair = (pieces[2 * k - 2], pieces[2 * k - 1], pairs[k - 1][2], rows)
            return piece_copies(table_ref, pair, weights.at[slot], sems.at[slot]) + [
                pltpu.make_async_copy(qkvs[k - 1], projected.at[slot], saved_sems.at[slot])
            ]

        def ahead_of(group):
            return lax.rem(group - me_ref[0] + parts, parts)

        def fetch(group, slot):
            for k in range(1, parts):

                @pl.when(ahead_of(group) == k)
                def _():
                    for c in copies(k, slot):
                        c.start()

        fetch(0, 0)
        d_first[...] = jnp.zeros_like(d_first)
        fill_bias(bias, staged.get(1), staged.get(2))
        branch_grad, own_grad, near_grad, own_weights = [staged.get(n) for n in (0, 3, 4, 5)]

        def group_step(group, carry):
            slot = lax.rem(group, 2)

            @pl.when(group < parts - 1)
            def _():
                fetch(group + 1, 1 - slot)

            used = weights.at[slot]

            @pl.when(ahead_of(group) == 0)
            def _():
                d_projected[...] = own_grad[...]
                used[: 3 * width] = own_weights[...]

            @pl.when(ahead_of(group) != 0)
            def _():
                for c in copies(1, slot):
                    c.wait()

            @pl.when(ahead_of(group) == 1)
            def _():
                d_projected[...] = near_grad[...]

            @pl.when(ahead_of(group) > 1)
            def _():
                d_attended[...] = dot_nt(branch_grad[...], used[3 * width :]).astype(LOW)
                head_gradients(
                    projected.at[slot], d_attended, bias, low_probs, d_scores, d_projected
                )

            d_first[...] += dot_nn(d_projected[...], used[: 3 * width])
            return carry

        lax.fori_loop(0, parts, group_step, 0)
        total = jnp.zeros(sums.shape, F32)
        step = length // 4
        chosen, turned, modulation_ref, tokens_ref, middle_ref = [
            staged.get(n) for n in (6, 7, 8, 9, 10)
        ]
        for r in range(4):
            block = slice(r * step, (r + 1) * step)
            normed, inverse = normalize_rows(tokens_ref[block].astype(F32))
            scale = modulate(chosen[block], modulation_ref, 1)
            grad = d_first[block]
            d_tokens[block] = middle_ref[block].astype(F32) + normalize_back(
                grad * (1.0 + scale), normed, inverse
            )
            total = total + jnp.concatenate(
                [split_sum(turned[:, block], v) for v in (grad, grad * normed)], 1
            )
        sums[...] = total

    return staged_call(
        body,
        [me, table],
        [
            d_branch,
            seg_col,
            seg_row,
            d_local,
            d_near,
            w_qkv,
            hot,
            hot_rows,
            modulation,
            tokens,
            d_middle,
        ],
        [shaped((length, model), F32), shaped((hot_rows.shape[0], 2 * model), F32)],
        "back_remote",
        52,
        raw=[p for pair in pairs for p in pair[:2]] + list(saved),
        scratch=back_scratch(length, width)
        + [
            pltpu.VMEM((2, 4 * width, model), LOW),
            pltpu.VMEM((2, length, 3 * width), LOW),
            pltpu.VMEM((length, 3 * width), LOW),
            pltpu.VMEM((length, model), F32),
            pltpu.SemaphoreType.DMA((2, PIECES)),
            pltpu.SemaphoreType.DMA((2,)),
        ],
    )


def mod_gradient(me, attn_sums, mlp_sums, rest, w_ada_rows, conds):
    wide, model = w_ada_rows.shape
    parts = len(mlp_sums)
    count = attn_sums.shape[0]

    def body(scalars, staged, raw, scratch):
        packed, product = staged.outs
        held = scratch[0]
        low = staged.get(0)
        total = [staged.get(1 + n)[...] for n in range(parts)]
        while len(total) > 1:
            total = [a + b for a, b in zip(total[0::2], total[1::2])]
        held[:, : low.shape[1]] = low[...]
        held[:, low.shape[1] :] = total[0]
        packed[...] = staged.get(1 + parts)[...]
        for k in range(held.shape[1] // wide):

            @pl.when(scalars[0][0] == k)
            def _():
                packed[:conds] = (
                    held[:conds, k * wide : (k + 1) * wide].astype(LOW).astype(F32)
                )

        staged.put(0)
        product[...] = dot_nn(packed[:count].astype(LOW), staged.get(2 + parts)[...])

    return staged_call(
        body,
        [me],
        [attn_sums, *mlp_sums, rest, w_ada_rows],
        [shaped(rest.shape, F32), shaped((count, model), F32)],
        "mod_gradient",
        24,
        scratch=[pltpu.VMEM((count, 6 * model), F32)],
    )


def factors(place, blocks, columns, units, model, conds):
    wide = blocks[0].shape[2]

    def body(scalars, staged, raw, scratch):
        d_w_ada, d_b_ada, d_b_out, d_b_up, d_b_down = staged.outs

        def pair_up(values_in):
            while len(values_in) > 1:
                values_in = [a + b for a, b in zip(values_in[0::2], values_in[1::2])]
            return values_in[0]

        each = [
            staged.get(k).at[n] for k in range(len(blocks)) for n in range(blocks[k].shape[0])
        ]
        d_mod = [one[:conds] for one in each]
        d_b_ada[...] = jnp.sum(pair_up(d_mod), 0)
        biases = pair_up([one[2 * conds :] for one in each])
        d_b_out[...] = biases[0, :model]
        d_b_up[...] = biases[1, :units]
        d_b_down[...] = biases[2, :model]
        row = lax.broadcasted_iota(jnp.int32, (model, columns), 0)
        column = lax.broadcasted_iota(jnp.int32, (model, columns), 1)
        pick = (row == column + scalars[0][0] * columns).astype(LOW)
        cond = jnp.concatenate([one[conds : 2 * conds, :model] for one in each], 0).astype(LOW)
        mine = dot_nn(cond, pick).astype(LOW)
        d_w_ada[...] = dot_tn(mine, jnp.concatenate(d_mod, 0).astype(LOW))

    return staged_call(
        body,
        [place],
        list(blocks),
        [
            shaped((columns, wide), F32),
            shaped((wide,), F32),
            shaped((model,), F32),
            shaped((units,), F32),
            shaped((model,), F32),
        ],
        "factors",
        32,
    )


def shards(
    tokens,
    conditioning,
    segments,
    crop_cond,
    w_ada,
    b_ada,
    w_qkv,
    w_out,
    b_out,
    w_up,
    b_up,
    w_down,
    b_down,
    d_out,
):
    length, width = tokens.shape
    cond_count = conditioning.shape[1]
    crop_count = crop_cond.shape[1]
    local_width = w_qkv.shape[2]
    parts = lax.axis_size("tensor")
    dp_count = lax.axis_size("dp")
    me = lax.axis_index("tensor")
    dp_me = lax.axis_index("dp")
    share = length // parts

    def from_ahead(value, step):
        return lax.ppermute(value, "tensor", [(s, (s - step) % parts) for s in range(parts)])

    def tensor_swap(value, distance):
        return lax.ppermute(value, "tensor", [(s, s ^ distance) for s in range(parts)])

    def dp_swap(value, distance):
        return lax.ppermute(value, "dp", [(s, s ^ distance) for s in range(dp_count)])

    steps = sorted(range(1, parts), key=lambda k: (-min(k, parts - k), k))

    def exchange(blocks):
        return lax.all_to_all(blocks, "tensor", 0, 0, tiled=True)

    levels = []
    left = dp_count
    stride = 1
    while left > 1:
        radix = 2 if (left % 4 or left == dp_count) and left % 2 == 0 else 4
        levels.append((stride, radix))
        stride *= radix
        left //= radix

    high = width // dp_count
    fast = [radix for _, radix in levels[:2]] == [2, dp_count // 2] and high % 16 == 0
    halves = (dp_count // 2, high) if fast else None
    dp_digit = dp_me % 2

    def dp_first(made):
        if fast:
            keep, send = made
            got = dp_swap(send, 1)
            return level_sum((dp_me // 2).reshape(1), keep, got)
        return (dp_level(made[0].reshape(dp_count, high, -1), levels[0], dp_count),)

    def dp_level(current, level, remaining):
        stride, radix = level
        digit = (dp_me // stride) % radix
        view = current.reshape((remaining // radix, radix) + current.shape[1:])
        total = lax.dynamic_index_in_dim(view, digit, 1, False).astype(F32)
        for m in sorted(range(1, radix), reverse=True):
            piece = lax.dynamic_index_in_dim(view, digit ^ m, 1, False).astype(LOW)
            total = total + dp_swap(piece, m * stride).astype(F32)
        return total

    def dp_rest(blocks, types):
        if fast:
            own, others = blocks[0], blocks[1:]
            got = [dp_swap(one, 2 * m) for m, one in enumerate(others, 1)]
            return finish_sum(own, got, types)
        (current,) = blocks
        remaining = current.shape[0]
        for level in levels[1:]:
            current = dp_level(current, level, remaining)
            remaining //= level[1]
        return finish_sum(current[0], [], types)

    def dp_gather(value):
        current = [value[None]]
        for stride, radix in levels:
            joined = current[0] if len(current) == 1 else jnp.concatenate(current)
            current = [joined] + [dp_swap(joined, m * stride) for m in range(1, radix)]
        return current

    def pair_sum(values_in):
        while values_in.shape[0] > 1:
            values_in = values_in[0::2] + values_in[1::2]
        return values_in[0]

    barrier = lax.optimization_barrier
    me_ref = me.reshape(1)
    cond_act, silu_back = jax.vjp(jax.nn.silu, conditioning.astype(F32))
    cond_low = cond_act.astype(LOW).reshape(cond_count, width)
    mod_part = (
        jnp.dot(cond_low, w_ada, preferred_element_type=F32) + b_ada.astype(F32)
    ).astype(LOW)
    mod_blocks = [mod_part] + [None] * (parts - 1)
    for k in steps:
        mod_blocks[k] = from_ahead(mod_part, k)
    in_place = []
    for j in range(parts):
        one = mod_blocks[0]
        for k in range(1, parts):
            one = jnp.where((me + k) % parts == j, mod_blocks[k], one)
        in_place.append(one)
    modulation = jnp.pad(jnp.concatenate(in_place, 1), ((0, HOT - cond_count), (0, 0)))

    rows = 4 * local_width // PIECES
    slot = dp_me % PIECES
    qkv_rows = w_qkv.transpose(1, 2, 0).reshape(3 * local_width, width)
    out_rows = w_out.T
    start = slot * rows
    piece = jnp.where(
        start < 3 * local_width,
        lax.dynamic_slice_in_dim(
            qkv_rows, jnp.minimum(start, 3 * local_width - rows), rows, 0
        ),
        lax.dynamic_slice_in_dim(out_rows, jnp.maximum(start - 3 * local_width, 0), rows, 0),
    )
    table = slot ^ jnp.array(
        [2 * a + c for c in (0, 1) for a in range(PIECES // 2)], jnp.int32
    )
    in_order = jnp.arange(PIECES, dtype=jnp.int32)
    order = [1] + list(range(parts - 1, 1, -1))
    pairs = [
        (qkv_rows.reshape(-1, rows, width), out_rows.reshape(-1, rows, width), 0)
    ] + [None] * (parts - 1)
    arrived = from_ahead(piece, order[0])

    seg_col = segments.reshape(length, 1)
    crop_match = seg_col == jnp.arange(crop_count, dtype=jnp.int32)[None, :]
    token_cond = jnp.sum(jnp.where(crop_match, crop_cond.reshape(1, crop_count), 0), -1)
    hot = (token_cond[:, None] == jnp.arange(HOT, dtype=jnp.int32)[None, :]).astype(LOW)
    hot_rows = (token_cond[None, :] == jnp.arange(HOT, dtype=jnp.int32)[:, None]).astype(LOW)

    def per_token(index, chosen):
        return jnp.dot(
            chosen,
            modulation[:, index * width : (index + 1) * width],
            preferred_element_type=F32,
        )

    def pass_on(block):
        return [block] + [dp_swap(block, 2 * m) for m in range(1, PIECES // 2)]

    def finish(passed):
        near = jnp.stack(passed)
        return (near, dp_swap(near, 1))

    second_z = from_ahead(piece, order[1])
    modulation, arrived, second_z, piece = barrier((modulation, arrived, second_z, piece))
    nearest = jnp.stack([arrived, second_z])
    passed = pass_on(nearest)
    last_z = from_ahead(piece, order[2])
    resid_in = tokens.astype(F32)
    normed_attn, _ = normalize_rows(resid_in)
    first_in = (normed_attn * (1.0 + per_token(1, hot)) + per_token(0, hot)).astype(LOW)
    saved = [None] * parts
    attended = [None] * parts
    w_outs = [None] * parts

    def group(k, chosen_table):
        saved[k], attended[k], w_outs[k] = attend_group(
            chosen_table, first_in, seg_col, segments, pairs[k], local_width
        )

    group(0, in_order)
    attended[0], last_z, grad_in = barrier((attended[0], last_z, d_out))
    last = pass_on(last_z)
    d_mixed = (grad_in.astype(F32) * per_token(5, hot)).astype(LOW)
    d_b_down = jnp.sum(d_mixed.astype(F32), 0)
    d_hidden = jnp.dot(d_mixed, w_down, preferred_element_type=F32)
    d_hidden, passed = barrier((d_hidden, passed))
    both = finish([one.reshape(2 * rows, width) for one in passed])
    for n, k in enumerate(order[:2]):
        pairs[k] = both + (n,)
        group(k, table)
    attended[order[1]], last = barrier((attended[order[1]], last))
    pairs[order[2]] = finish(last) + (0,)
    group(order[2], table)
    branch, middle, second_in, hidden, d_pre, d_second_parts, d_b_up = mlp_forward(
        me_ref,
        attended,
        w_outs,
        b_out.astype(F32).reshape(1, width),
        tokens,
        hot,
        modulation,
        d_hidden,
        w_up,
        b_up.astype(F32).reshape(1, -1),
    )
    second_arrived = exchange(d_second_parts)

    mlp_low, gate_sums = mlp_down(hidden, w_down, d_out, hot_rows, parts)
    digit_ref = dp_digit.reshape(1)
    mlp_made = mlp_grads(digit_ref, d_mixed, hidden, second_in, d_pre, halves)
    second_arrived, mlp_made, mlp_low, gate_sums = barrier(
        (second_arrived, mlp_made, mlp_low, gate_sums)
    )
    spread, d_second, d_middle_own = turn_back(
        me_ref, second_arrived, modulation, middle, d_out, hot
    )
    d_middle = exchange(spread).reshape(length, width)

    mlp_blocks = dp_first(mlp_made)
    d_middle, mlp_blocks, mlp_low = barrier((d_middle, mlp_blocks, mlp_low))
    d_w_down, d_w_up = dp_rest(mlp_blocks, [shaped((high, w_down.shape[1]), F32)] * 2)
    mlp_arrived = exchange(mlp_low)
    d_branch, d_local, d_near, *attention_parts, d_b_out = back_first(
        digit_ref,
        d_middle,
        hot,
        modulation,
        seg_col,
        segments,
        out_rows,
        saved[0],
        first_in,
        attended[0],
        w_outs[1],
        saved[1],
        halves,
    )
    d_branch, attention_parts, mlp_arrived, d_w_down, d_w_up, d_second = barrier(
        (d_branch, attention_parts, mlp_arrived, d_w_down, d_w_up, d_second)
    )
    b_down_row = b_down.astype(F32).reshape(1, width)
    output_parts = output_rows(me_ref, mlp_arrived, b_down_row, middle, modulation, hot)
    output = exchange(output_parts).reshape(length, width)
    attention_blocks = dp_first(attention_parts)
    mlp_sums = own_sums(
        me_ref, branch, middle, d_second, d_middle_own, d_out, b_down_row, hot_rows, gate_sums
    )
    mlp_all = [mlp_sums] + [tensor_swap(mlp_sums, m) for m in range(1, parts)]
    d_branch, output_parts, attention_blocks, mlp_sums = barrier(
        (d_branch, output_parts, attention_blocks, mlp_sums)
    )
    d_tokens, attn_sums = back_remote(
        me_ref,
        table,
        d_branch,
        seg_col,
        segments,
        d_local,
        d_near,
        qkv_rows,
        hot,
        hot_rows,
        modulation,
        tokens,
        d_middle,
        pairs[1:],
        saved[1:],
    )
    d_w_qkv, d_w_out = dp_rest(
        attention_blocks,
        [shaped((3, high, local_width), F32), shaped((high, local_width), F32)],
    )
    d_w_qkv = d_w_qkv.transpose(1, 0, 2)
    attn_sums, output, d_w_qkv, d_w_out, mlp_all = barrier(
        (attn_sums, output, d_w_qkv, d_w_out, mlp_all)
    )
    mod_width = w_ada.shape[1]

    def row(values_in):
        flat = values_in.reshape(-1, values_in.shape[-1]).astype(F32)
        return jnp.pad(flat, ((0, 0), (0, mod_width - flat.shape[1])))

    others = jnp.concatenate(
        [jnp.zeros((cond_count, mod_width), F32)]
        + [row(one) for one in (cond_low, d_b_out, d_b_up, d_b_down[None])]
        + [jnp.zeros((5, mod_width), F32)]
    )
    packed, d_silu_part = mod_gradient(
        me_ref, attn_sums, mlp_all, others, w_ada.T, cond_count
    )
    gathered = dp_gather(packed)
    d_silu = pair_sum(
        jnp.stack([d_silu_part] + [tensor_swap(d_silu_part, m) for m in range(1, parts)])
    )[:cond_count]
    d_conditioning = silu_back(d_silu.reshape(conditioning.shape))[0]
    d_w_ada, d_b_ada, d_b_out, d_b_up, d_b_down = factors(
        dp_me.reshape(1), gathered, width // dp_count, d_b_up.shape[1], width, cond_count
    )
    return (
        output,
        d_tokens,
        d_conditioning,
        d_w_ada,
        d_b_ada,
        d_w_qkv,
        d_w_out,
        d_b_out,
        d_w_up,
        d_b_up,
        d_w_down,
        d_b_down,
    )


def solution(mesh):
    return jax.shard_map(
        shards,
        mesh=mesh,
        in_specs=(
            P("dp", None),
            P("dp", None, None),
            P("dp", None),
            P("dp", None),
            P(None, "tensor"),
            P("tensor"),
            P(None, None, "tensor"),
            P(None, "tensor"),
            P(),
            P(None, "tensor"),
            P("tensor"),
            P(None, "tensor"),
            P(),
            P("dp", None),
        ),
        out_specs=(
            P("dp", None),
            P("dp", None),
            P("dp", None, None),
            P("dp", "tensor"),
            P("tensor"),
            P("dp", None, "tensor"),
            P("dp", "tensor"),
            P(),
            P("dp", "tensor"),
            P("tensor"),
            P("dp", "tensor"),
            P(),
        ),
        check_vma=False,
    )
```

```python
import jax
import jax.numpy as jnp
from jax import lax
from jax.experimental import pallas as pl
from jax.experimental.pallas import tpu as pltpu
from jax.sharding import PartitionSpec as P

HD = 72
F32 = jnp.float32
LOW = jnp.bfloat16
NEG = -1e30
LOG2E = 1.4426950408889634
PIECES = 8
HOT = 8
SMEM = pl.BlockSpec(memory_space=pltpu.SMEM)
HBM = pl.BlockSpec(memory_space=pltpu.HBM)
SMALL = pl.CostEstimate(flops=1 << 20, transcendentals=0, bytes_accessed=1 << 20)


def dot_nn(a, b):
    return lax.dot_general(a, b, (((1,), (0,)), ((), ())), preferred_element_type=F32)


def dot_nt(a, b):
    return lax.dot_general(a, b, (((1,), (1,)), ((), ())), preferred_element_type=F32)


def dot_tn(a, b):
    return lax.dot_general(a, b, (((0,), (0,)), ((), ())), preferred_element_type=F32)


def normalize_rows(values):
    average = jnp.mean(values, -1, keepdims=True)
    centered = values - average
    variance = jnp.mean(centered * centered, -1, keepdims=True)
    inverse = lax.rsqrt(variance + 1e-06)
    return (centered * inverse, inverse)


def normalize_back(gradient, normed, inverse):
    return inverse * (
        gradient
        - jnp.mean(gradient, -1, keepdims=True)
        - normed * jnp.mean(gradient * normed, -1, keepdims=True)
    )


def softmax_rows(queries, key_vecs, bias):
    scaled = dot_nt(queries, key_vecs) * (HD**-0.5 * LOG2E) + bias
    exponent = jnp.exp2(scaled - jnp.max(scaled, -1, keepdims=True))
    return exponent * (1.0 / jnp.sum(exponent, -1, keepdims=True))


def piece_copies(table, pair, into, sems):
    first, second, step, rows = pair
    ahead = first.shape[0]
    copies = []
    for n in range(PIECES):
        source = first.at[n] if n < ahead else second.at[n - ahead]
        source = source.at[step * rows : (step + 1) * rows, :]
        place = pl.ds(pl.multiple_of(table[n] * rows, 16), rows)
        copies.append(pltpu.make_async_copy(source, into.at[place, :], sems.at[n]))
    return copies


class Staged:
    def __init__(self, sources, ins, in_sems, outs, targets, out_sems):
        self.coming = [
            pltpu.make_async_copy(a, b, in_sems.at[n])
            for n, (a, b) in enumerate(zip(sources, ins))
        ]
        self.going = [[] for _ in outs]
        self.ins, self.outs = ins, outs
        self.here = set()
        self.pairs, self.out_sems = list(zip(outs, targets)), out_sems
        for one in self.coming:
            one.start()

    def get(self, n):
        if n not in self.here:
            self.here.add(n)
            self.coming[n].wait()
        return self.ins[n]

    def put(self, n):
        one = pltpu.make_async_copy(*self.pairs[n], self.out_sems.at[n])
        one.start()
        self.going[n].append(one)

    def put_part(self, n, part, parts, size):
        source, target = self.pairs[n]
        place = slice(part * size, (part + 1) * size)
        one = pltpu.make_async_copy(
            source.at[place], target.at[place], self.out_sems.at[len(self.pairs) * (1 + part) + n]
        )
        one.start()
        self.going[n].append(one)

    def finish(self):
        for n in range(len(self.coming)):
            self.get(n)
        for n, made in enumerate(self.going):
            if not made:
                self.put(n)
        for made in self.going:
            for one in made:
                one.wait()


OWN_ROWS = "rows"
OWN_FREE = "rows anywhere"
FREE = "anywhere"
OWN_COLUMNS = "columns"


def staged_call(
    body, scalars, ins, outs, name, mib, raw=(), raw_outs=(), scratch=(), small=True, share=0
):
    plain = [one if isinstance(one, tuple) else (one, None) for one in ins]
    arrays = [
        one if kind in (FREE, OWN_FREE) else pltpu.with_memory_space_constraint(one, pltpu.HBM)
        for one, kind in plain
    ]
    shapes = []
    for one, kind in plain:
        shape = list(one.shape)
        if kind in (OWN_ROWS, OWN_FREE):
            shape[0] = share
        if kind == OWN_COLUMNS:
            shape[1] = share
        shapes.append(pltpu.VMEM(tuple(shape), one.dtype))
    counts = [
        len(scalars),
        len(ins),
        len(raw),
        len(outs),
        len(raw_outs),
        len(ins),
        len(outs),
    ]

    def kernel(*refs):
        groups, at = [], 0
        for count in counts:
            groups.append(refs[at : at + count])
            at += count
        scalar_refs, sources, raw_refs, targets, raw_targets, in_refs, out_refs = groups
        in_sems, out_sems = refs[at : at + 2]
        picked = []
        for source, (_, kind) in zip(sources, plain):
            if kind in (OWN_ROWS, OWN_FREE):
                source = source.at[pl.ds(pl.multiple_of(scalar_refs[0][0] * share, 16), share), :]
            if kind == OWN_COLUMNS:
                source = source.at[:, pl.ds(pl.multiple_of(scalar_refs[0][0] * share, 128), share)]
            picked.append(source)
        staged = Staged(picked, in_refs, in_sems, out_refs, targets, out_sems)
        body(scalar_refs, staged, raw_refs + raw_targets, refs[at + 2 :])
        staged.finish()

    return pl.pallas_call(
        kernel,
        out_shape=tuple(pltpu.HBM(one.shape, one.dtype) for one in (*outs, *raw_outs)),
        in_specs=[SMEM] * len(scalars) + [HBM] * (len(ins) + len(raw)),
        out_specs=(HBM,) * (len(outs) + len(raw_outs)),
        scratch_shapes=shapes
        + [pltpu.VMEM(one.shape, one.dtype) for one in outs]
        + [pltpu.SemaphoreType.DMA((len(ins),)), pltpu.SemaphoreType.DMA((3 * max(len(outs), 1),))]
        + list(scratch),
        compiler_params=pltpu.CompilerParams(vmem_limit_bytes=mib << 20),
        cost_estimate=SMALL if small else None,
        name=name,
    )(*scalars, *arrays, *raw)


def shaped(shape, dtype):
    return jax.ShapeDtypeStruct(shape, dtype)


def modulate(hot, modulation, index):
    model = modulation.shape[1] // 6
    return dot_nn(hot[...], modulation[:, index * model : (index + 1) * model])


def fill_bias(bias, seg_col, seg_row):
    bias[...] = jnp.where(seg_col[...] == seg_row[...], 0.0, NEG)


def attend_group(table, first_in, seg_col, seg_row, pair, width):
    length, model = first_in.shape
    total = 4 * width

    def body(scalars, staged, raw, scratch):
        weights, bias, sems = scratch
        pieces = piece_copies(scalars[0], (*raw, pair[2], total // PIECES), weights, sems)
        for c in pieces:
            c.start()
        fill_bias(bias, staged.get(1), staged.get(2))
        projected, attended, w_out = staged.outs
        for c in pieces:
            c.wait()
        projected[...] = dot_nt(staged.get(0)[...], weights[: 3 * width]).astype(LOW)
        staged.put(0)
        w_out[...] = weights[3 * width :]
        staged.put(2)
        for h in range(width // HD):
            queries, key_vecs, values = [
                projected[:, j * width + h * HD : j * width + (h + 1) * HD] for j in range(3)
            ]
            probs = softmax_rows(queries, key_vecs, bias[...])
            attended[:, h * HD : (h + 1) * HD] = dot_nn(probs.astype(LOW), values).astype(LOW)

    return staged_call(
        body,
        [table],
        [(first_in, FREE), (seg_col, FREE), (seg_row, FREE)],
        [
            shaped((length, 3 * width), LOW),
            shaped((length, width), LOW),
            shaped((width, model), LOW),
        ],
        "attend_group",
        32,
        raw=pair[:2],
        scratch=[
            pltpu.VMEM((total, model), LOW),
            pltpu.VMEM((length, length), F32),
            pltpu.SemaphoreType.DMA((PIECES,)),
        ],
    )


def head_gradients(qkv, d_attended, bias, low_probs, d_scores, d_projected):
    width = d_attended.shape[1]
    scale = HD**-0.5
    for h in range(width // HD):
        columns = slice(h * HD, (h + 1) * HD)
        queries, key_vecs, values = [
            qkv[:, j * width + h * HD : j * width + (h + 1) * HD] for j in range(3)
        ]
        d_head = d_attended[:, columns]
        probs = softmax_rows(queries, key_vecs, bias[...])
        d_probs = dot_nt(d_head, values)
        inner = jnp.sum(d_probs * probs, -1, keepdims=True)
        low_probs[h] = probs.astype(LOW)
        d_scores[h] = (probs * (d_probs - inner)).astype(LOW)
        d_projected[:, h * HD : (h + 1) * HD] = (dot_nn(d_scores[h], key_vecs) * scale).astype(
            LOW
        )
        d_projected[:, width + h * HD : width + (h + 1) * HD] = (
            dot_tn(d_scores[h], queries) * scale
        ).astype(LOW)
        d_projected[:, 2 * width + h * HD : 2 * width + (h + 1) * HD] = dot_tn(
            low_probs[h], d_head
        ).astype(LOW)


def split_sum(hot_rows, values_in):
    high = values_in.astype(LOW)
    rest = values_in - high.astype(F32)
    mid = rest.astype(LOW)
    low = (rest - mid.astype(F32)).astype(LOW)
    return dot_nn(hot_rows, high) + dot_nn(hot_rows, mid) + dot_nn(hot_rows, low)


def mlp_forward(me, attended, w_out, b_out, tokens, hot, modulation, d_hidden, w_up, b_up):
    parts = len(attended)
    length, model = tokens.shape
    units = w_up.shape[1]
    share = length // parts

    def body(scalars, staged, raw, scratch):
        held = scratch[0]
        own_branch, own_middle, second_in, hidden, d_pre, d_second, d_b_up = staged.outs
        rows = length // 2
        sums = jnp.zeros((1, units), F32)
        for step in range(2):
            block = slice(step * rows, (step + 1) * rows)
            branch = staged.get(2 * parts)[...]
            for k in range(parts):
                branch = branch + dot_nn(staged.get(k)[block], staged.get(parts + k)[...])
            chosen, table = staged.get(2 * parts + 2)[block], staged.get(2 * parts + 3)
            stream = staged.get(2 * parts + 1)[block].astype(F32) + (
                modulate(chosen, table, 2) * branch
            )
            held[0, block] = branch
            held[1, block] = stream
            normed, _ = normalize_rows(stream)
            second = (normed * (1.0 + modulate(chosen, table, 4)) + modulate(chosen, table, 3)).astype(LOW)
            second_in[block] = second
            staged.put_part(2, step, 2, rows)
            weights = staged.get(2 * parts + 5)
            u = dot_nn(second, weights[...]) + staged.get(2 * parts + 6)[...]
            root = 0.7978845608028654
            square = u * u
            bent = jnp.tanh(root * u * (1.0 + 0.044715 * square))
            half = 0.5 * (1.0 + bent)
            hidden[block] = (u * half).astype(LOW)
            staged.put_part(3, step, 2, rows)
            slope = half + 0.5 * u * (1.0 - bent * bent) * (root * (1.0 + 3 * 0.044715 * square))
            low = (staged.get(2 * parts + 4)[block] * slope).astype(LOW)
            d_pre[block] = low
            staged.put_part(4, step, 2, rows)
            sums = sums + jnp.sum(low.astype(F32), 0, keepdims=True)
            added = dot_nt(low, weights[...]).astype(LOW)
            for n in range(rows // share):
                d_second[step * (rows // share) + n] = added[n * share : (n + 1) * share]
            staged.put_part(5, step, 2, rows // share)
        d_b_up[...] = sums
        mine = pl.ds(pl.multiple_of(scalars[0][0] * share, 8), share)
        own_branch[...] = held[0, mine, :]
        own_middle[...] = held[1, mine, :]

    return staged_call(
        body,
        [me],
        [*attended, *w_out, (b_out, FREE), tokens, (hot, FREE), (modulation, FREE), (d_hidden, FREE), w_up, (b_up, FREE)],
        [
            shaped((share, model), F32),
            shaped((share, model), F32),
            shaped((length, model), LOW),
            shaped((length, units), LOW),
            shaped((length, units), LOW),
            shaped((parts, share, model), LOW),
            shaped((1, units), F32),
        ],
        "mlp_forward",
        48,
        scratch=[pltpu.VMEM((2, length, model), F32)],
        small=False,
    )


def mlp_down(hidden, w_down, d_out, hot_rows, parts):
    length, model = d_out.shape
    share = length // parts
    count = hot_rows.shape[0]

    def body(scalars, staged, raw, scratch):
        low, sums = staged.outs
        total = jnp.zeros((count, model), F32)
        rows = length // 2
        for step in range(2):
            block = slice(step * rows, (step + 1) * rows)
            added = dot_nt(staged.get(0)[block], staged.get(1)[...])
            for n in range(rows // share):
                low[step * (rows // share) + n] = added[n * share : (n + 1) * share].astype(LOW)
            staged.put_part(0, step, 2, rows // share)
            total = total + split_sum(
                staged.get(3)[:, block], staged.get(2)[block].astype(F32) * added
            )
        sums[...] = total

    return staged_call(
        body,
        [],
        [hidden, w_down, d_out, (hot_rows, FREE)],
        [shaped((parts, share, model), LOW), shaped((count, model), F32)],
        "mlp_down",
        32,
    )


def hand_out_types(halves, rows, columns):
    if halves is None:
        return [shaped((rows, columns), F32)]
    count, high = halves
    return [shaped((count, high, columns), F32)] + [shaped((high, columns), LOW)] * count


def hand_out(digit, whole, outs):
    if len(outs) == 1:
        outs[0][...] = whole[...]
        return
    keep, *send = outs
    high = keep.shape[1]
    for n, one in enumerate(send):
        keep[n] = whole[pl.ds(pl.multiple_of((2 * n + digit) * high, 8), high), :]
        one[...] = whole[pl.ds(pl.multiple_of((2 * n + 1 - digit) * high, 8), high), :].astype(LOW)


def mlp_grads(digit, d_mixed, hidden, second_in, d_pre, halves):
    model, units = d_mixed.shape[1], hidden.shape[1]

    def body(scalars, staged, raw, scratch):
        whole = scratch[0]
        whole[:, :units] = dot_tn(staged.get(0)[...], staged.get(1)[...])
        whole[:, units:] = dot_tn(staged.get(2)[...], staged.get(3)[...])
        hand_out(scalars[0][0], whole, staged.outs)

    return staged_call(
        body,
        [digit],
        [(d_mixed, FREE), hidden, second_in, d_pre],
        hand_out_types(halves, model, 2 * units),
        "mlp_grads",
        48,
        scratch=[pltpu.VMEM((model, 2 * units), F32)],
    )


def level_sum(digit, keep, got, earlier=(), cut=0):
    radix, rows, columns = keep.shape
    before = earlier[0].shape[1] if earlier else 0
    widths = [cut, columns - cut] if cut else [before + columns]

    def body(scalars, staged, raw, scratch):
        came = scratch[0]
        mine = scalars[0][0]
        for n in range(radix):
            came[n] = staged.get(1 + n)[...]
        kept = staged.get(0)
        for m in range(1, radix):
            other = jnp.bitwise_xor(mine, m)
            total = (kept[other] + came[other].astype(F32)).astype(LOW)
            if cut:
                staged.outs[m][...] = total[:, :cut]
                staged.outs[radix - 1 + m][...] = total[:, cut:]
                staged.put(radix - 1 + m)
            else:
                if earlier:
                    staged.outs[m][:, :before] = staged.get(radix + m)[...]
                staged.outs[m][:, before:] = total
            staged.put(m)
        staged.outs[0][...] = kept[mine] + came[mine].astype(F32)

    return staged_call(
        body,
        [digit],
        [keep, *[(one, FREE) for one in got], *earlier],
        [shaped((rows, columns), F32)]
        + [shaped((rows, wide), LOW) for wide in widths for _ in range(radix - 1)],
        "level_sum",
        40,
        scratch=[pltpu.VMEM(keep.shape, LOW)],
    )


def finish_sum(owns, got, types):
    def body(scalars, staged, raw, scratch):
        n, at, base, total = 0, 0, 0, None
        for out in staged.outs:
            width = out.shape[-1]
            for j in range(out.shape[0] if len(out.shape) == 3 else 1):
                if total is None:
                    _, begin, wide = owns[n]
                    total = staged.get(n)[:, begin : begin + wide]
                    for k in range(len(got)):
                        total = total + staged.get(len(owns) + k)[:, base : base + wide].astype(F32)
                target = out.at[j] if len(out.shape) == 3 else out
                target[...] = total[:, at : at + width]
                at += width
                if at == wide:
                    n, at, base, total = n + 1, 0, base + wide, None

    return staged_call(
        body, [], [*[one[0] for one in owns], *[(one, FREE) for one in got]], types, "finish_sum", 32
    )


def turn_back(me, arrived, modulation, middle, d_out, hot):
    parts, share, model = arrived.shape

    def body(scalars, staged, raw, scratch):
        spread, d_second, d_middle = staged.outs
        normed, inverse = normalize_rows(staged.get(2)[...])
        scale = modulate(staged.get(4), staged.get(1), 4)
        came = staged.get(0)
        grad = came[0].astype(F32)
        for k in range(1, parts):
            grad = grad + came[k].astype(F32)
        d_second[...] = grad
        moved = staged.get(3)[...].astype(F32) + normalize_back(
            grad * (1.0 + scale), normed, inverse
        )
        d_middle[...] = moved
        for k in range(parts):
            spread[k] = moved.astype(LOW)

    return staged_call(
        body,
        [me],
        [(arrived, FREE), (modulation, FREE), middle, (d_out, OWN_ROWS), (hot, OWN_FREE)],
        [
            shaped(arrived.shape, LOW),
            shaped((share, model), F32),
            shaped((share, model), F32),
        ],
        "turn_back",
        16,
        share=share,
    )


def output_rows(
    me,
    arrived,
    b_down,
    middle,
    modulation,
    hot,
    branch,
    d_second,
    d_middle,
    d_out,
    hot_rows,
    gate_sums,
    conds,
):
    parts, share, model = arrived.shape
    extra = 4 * conds

    def body(scalars, staged, raw, scratch):
        held = scratch[0]
        came = staged.get(0)
        total = staged.get(1)[...]
        for k in range(parts):
            total = total + came[k].astype(F32)
        made = staged.get(2)[...] + modulate(staged.get(4), staged.get(3), 5) * total
        normed, _ = normalize_rows(staged.get(2)[...])
        second, moved = staged.get(6), staged.get(7)
        each = [
            moved[...] * staged.get(5)[...],
            second[...],
            second[...] * normed,
            staged.get(8)[...].astype(F32) * staged.get(1)[...],
        ]
        for n, one in enumerate(each):
            added = split_sum(staged.get(9)[...], one)
            if n == len(each) - 1:
                added = added + staged.get(10)[...]
            held[n * conds : (n + 1) * conds] = added[:conds]
        high = held[...].astype(LOW)
        rest = (held[...] - high.astype(F32)).astype(LOW)
        low = made.astype(LOW)
        spread = staged.outs[0]
        for k in range(parts):
            spread[k, :share] = low
            spread[k, share : share + extra] = high
            spread[k, share + extra :] = rest

    return staged_call(
        body,
        [me],
        [
            (arrived, FREE),
            (b_down, FREE),
            middle,
            (modulation, FREE),
            (hot, OWN_FREE),
            branch,
            d_second,
            d_middle,
            (d_out, OWN_ROWS),
            (hot_rows, OWN_COLUMNS),
            (gate_sums, FREE),
        ],
        [shaped((parts, share + 2 * extra, model), LOW)],
        "output_rows",
        24,
        scratch=[pltpu.VMEM((extra, model), F32)],
        share=share,
    )[0]


def back_scratch(length, width):
    heads = width // HD
    return [
        pltpu.VMEM((length, width), LOW),
        pltpu.VMEM((heads, length, length), LOW),
        pltpu.VMEM((heads, length, length), LOW),
        pltpu.VMEM((length, length), F32),
    ]


def back_first(
    digit,
    d_middle,
    hot,
    modulation,
    seg_col,
    seg_row,
    w_out,
    qkv,
    first_in,
    attended,
    near_out,
    near_qkv,
    halves,
):
    length, model = d_middle.shape
    width = attended.shape[1]

    def body(scalars, staged, raw, scratch):
        d_attended, low_probs, d_scores, bias, whole = scratch
        d_branch, d_local, d_near, *outs, d_b_out = staged.outs
        gate = modulate(staged.get(1), staged.get(2), 2)
        d_branch[...] = (staged.get(0)[...].astype(F32) * gate).astype(LOW)
        staged.put(0)
        d_b_out[...] = jnp.sum(d_branch[...].astype(F32), 0, keepdims=True)
        fill_bias(bias, staged.get(3), staged.get(4))
        d_attended[...] = dot_nt(d_branch[...], staged.get(5)[...]).astype(LOW)
        head_gradients(staged.get(6), d_attended, bias, low_probs, d_scores, d_local)
        staged.put(1)
        whole[:, : 3 * width] = dot_tn(staged.get(7)[...], d_local[...])
        whole[:, 3 * width :] = dot_tn(d_branch[...], staged.get(8)[...])
        hand_out(scalars[0][0], whole, outs)
        for n in range(len(outs)):
            staged.put(3 + n)
        d_attended[...] = dot_nt(d_branch[...], staged.get(9)[...]).astype(LOW)
        head_gradients(staged.get(10), d_attended, bias, low_probs, d_scores, d_near)

    return staged_call(
        body,
        [digit],
        [
            (d_middle, FREE),
            (hot, FREE),
            (modulation, FREE),
            (seg_col, FREE),
            (seg_row, FREE),
            (w_out, FREE),
            qkv,
            (first_in, FREE),
            attended,
            near_out,
            near_qkv,
        ],
        [
            shaped((length, model), LOW),
            shaped((length, 3 * width), LOW),
            shaped((length, 3 * width), LOW),
            *hand_out_types(halves, model, 4 * width),
            shaped((1, model), F32),
        ],
        "back_first",
        52,
        scratch=back_scratch(length, width) + [pltpu.VMEM((model, 4 * width), F32)],
    )


def back_remote(
    me,
    table,
    d_branch,
    seg_col,
    seg_row,
    d_local,
    d_near,
    w_qkv,
    hot,
    hot_rows,
    modulation,
    tokens,
    d_middle,
    pairs,
    saved,
):
    length, model = d_branch.shape
    width = d_local.shape[1] // 3
    remote = len(saved)
    parts = remote + 1
    rows = 4 * width // PIECES

    def body(scalars, staged, raw, scratch):
        (
            d_attended,
            low_probs,
            d_scores,
            bias,
            weights,
            projected,
            d_projected,
            d_first,
            sems,
            saved_sems,
        ) = scratch
        me_ref, table_ref = scalars
        pieces, qkvs = raw[: 2 * remote], raw[2 * remote :]
        d_tokens, sums = staged.outs

        def copies(k, slot):
            pair = (pieces[2 * k - 2], pieces[2 * k - 1], pairs[k - 1][2], rows)
            return piece_copies(table_ref, pair, weights.at[slot], sems.at[slot]) + [
                pltpu.make_async_copy(qkvs[k - 1], projected.at[slot], saved_sems.at[slot])
            ]

        def ahead_of(group):
            return lax.rem(group - me_ref[0] + parts, parts)

        def fetch(group, slot):
            for k in range(1, parts):

                @pl.when(ahead_of(group) == k)
                def _():
                    for c in copies(k, slot):
                        c.start()

        fetch(0, 0)
        d_first[...] = jnp.zeros_like(d_first)
        fill_bias(bias, staged.get(1), staged.get(2))
        branch_grad, own_grad, near_grad, own_weights = [staged.get(n) for n in (0, 3, 4, 5)]

        def group_step(group, carry):
            slot = lax.rem(group, 2)

            @pl.when(group < parts - 1)
            def _():
                fetch(group + 1, 1 - slot)

            used = weights.at[slot]

            @pl.when(ahead_of(group) == 0)
            def _():
                d_projected[...] = own_grad[...]
                used[: 3 * width] = own_weights[...]

            @pl.when(ahead_of(group) != 0)
            def _():
                for c in copies(1, slot):
                    c.wait()

            @pl.when(ahead_of(group) == 1)
            def _():
                d_projected[...] = near_grad[...]

            @pl.when(ahead_of(group) > 1)
            def _():
                d_attended[...] = dot_nt(branch_grad[...], used[3 * width :]).astype(LOW)
                head_gradients(
                    projected.at[slot], d_attended, bias, low_probs, d_scores, d_projected
                )

            d_first[...] += dot_nn(d_projected[...], used[: 3 * width])
            return carry

        lax.fori_loop(0, parts, group_step, 0)
        total = jnp.zeros(sums.shape, F32)
        step = length // 4
        chosen, turned, modulation_ref, tokens_ref, middle_ref = [
            staged.get(n) for n in (6, 7, 8, 9, 10)
        ]
        for r in range(4):
            block = slice(r * step, (r + 1) * step)
            normed, inverse = normalize_rows(tokens_ref[block].astype(F32))
            scale = modulate(chosen[block], modulation_ref, 1)
            grad = d_first[block]
            d_tokens[block] = middle_ref[block].astype(F32) + normalize_back(
                grad * (1.0 + scale), normed, inverse
            )
            total = total + jnp.concatenate(
                [split_sum(turned[:, block], v) for v in (grad, grad * normed)], 1
            )
        sums[...] = total

    return staged_call(
        body,
        [me, table],
        [
            d_branch,
            (seg_col, FREE),
            (seg_row, FREE),
            d_local,
            d_near,
            w_qkv,
            (hot, FREE),
            (hot_rows, FREE),
            (modulation, FREE),
            tokens,
            (d_middle, FREE),
        ],
        [shaped((length, model), F32), shaped((hot_rows.shape[0], 2 * model), F32)],
        "back_remote",
        52,
        raw=[p for pair in pairs for p in pair[:2]] + list(saved),
        scratch=back_scratch(length, width)
        + [
            pltpu.VMEM((2, 4 * width, model), LOW),
            pltpu.VMEM((2, length, 3 * width), LOW),
            pltpu.VMEM((length, 3 * width), LOW),
            pltpu.VMEM((length, model), F32),
            pltpu.SemaphoreType.DMA((2, PIECES)),
            pltpu.SemaphoreType.DMA((2,)),
        ],
    )


def mod_gradient(me, attn_sums, arrived, rest, conds):
    parts, high, model = arrived.shape
    extra = 4 * conds
    share = high - 2 * extra
    wide = rest.shape[1]

    def body(scalars, staged, raw, scratch):
        came, output = raw
        held, tails, sems = scratch
        packed = staged.outs[0]
        below = pltpu.make_async_copy(came.at[:, share:, :], tails, sems.at[parts])
        below.start()
        copies = [
            pltpu.make_async_copy(
                came.at[k, :share, :], output.at[k * share : (k + 1) * share, :], sems.at[k]
            )
            for k in range(parts)
        ]
        for c in copies:
            c.start()
        low = staged.get(0)
        held[:, : low.shape[1]] = low[:conds]
        packed[...] = staged.get(1)[...]
        below.wait()
        total = jnp.zeros((extra, model), F32)
        for k in range(parts):
            total = total + (
                tails[k, :extra].astype(F32) + tails[k, extra : 2 * extra].astype(F32)
            )
        for n in range(4):
            held[:, (2 + n) * model : (3 + n) * model] = total[n * conds : (n + 1) * conds]
        for k in range(held.shape[1] // wide):

            @pl.when(scalars[0][0] == k)
            def _():
                packed[:conds] = held[:, k * wide : (k + 1) * wide].astype(LOW).astype(F32)

        for c in copies:
            c.wait()

    return staged_call(
        body,
        [me],
        [attn_sums, (rest, FREE)],
        [shaped(rest.shape, F32)],
        "mod_gradient",
        24,
        raw=[arrived],
        raw_outs=[shaped((parts * share, model), LOW)],
        scratch=[
            pltpu.VMEM((conds, 6 * model), F32),
            pltpu.VMEM((parts, 2 * extra, model), LOW),
            pltpu.SemaphoreType.DMA((parts + 1,)),
        ],
    )


def mod_product(joined, w_ada_rows):
    wide, model = w_ada_rows.shape

    def body(scalars, staged, raw, scratch):
        staged.outs[0][...] = dot_nn(staged.get(0)[0, :8].astype(LOW), staged.get(1)[...])

    return staged_call(
        body, [], [(joined, FREE), w_ada_rows], [shaped((8, model), F32)], "mod_product", 24
    )[0]


def factors(place, blocks, columns, units, model, conds):
    wide = blocks[0].shape[2]

    def body(scalars, staged, raw, scratch):
        d_w_ada, d_b_ada, d_b_out, d_b_up, d_b_down = staged.outs

        def pair_up(values_in):
            while len(values_in) > 1:
                values_in = [a + b for a, b in zip(values_in[0::2], values_in[1::2])]
            return values_in[0]

        each = [
            staged.get(k).at[n] for k in range(len(blocks)) for n in range(blocks[k].shape[0])
        ]
        d_mod = [one[:conds] for one in each]
        d_b_ada[...] = jnp.sum(pair_up(d_mod), 0)
        biases = pair_up([one[2 * conds :] for one in each])
        d_b_out[...] = biases[0, :model]
        d_b_up[...] = biases[1, :units]
        d_b_down[...] = biases[2, :model]
        row = lax.broadcasted_iota(jnp.int32, (model, columns), 0)
        column = lax.broadcasted_iota(jnp.int32, (model, columns), 1)
        pick = (row == column + scalars[0][0] * columns).astype(LOW)
        cond = jnp.concatenate([one[conds : 2 * conds, :model] for one in each], 0).astype(LOW)
        mine = dot_nn(cond, pick).astype(LOW)
        d_w_ada[...] = dot_tn(mine, jnp.concatenate(d_mod, 0).astype(LOW))

    return staged_call(
        body,
        [place],
        [(one, FREE) for one in blocks],
        [
            shaped((columns, wide), F32),
            shaped((wide,), F32),
            shaped((model,), F32),
            shaped((units,), F32),
            shaped((model,), F32),
        ],
        "factors",
        32,
    )


def shards(
    tokens,
    conditioning,
    segments,
    crop_cond,
    w_ada,
    b_ada,
    w_qkv,
    w_out,
    b_out,
    w_up,
    b_up,
    w_down,
    b_down,
    d_out,
):
    length, width = tokens.shape
    cond_count = conditioning.shape[1]
    crop_count = crop_cond.shape[1]
    local_width = w_qkv.shape[2]
    parts = lax.axis_size("tensor")
    dp_count = lax.axis_size("dp")
    me = lax.axis_index("tensor")
    dp_me = lax.axis_index("dp")
    share = length // parts

    def from_ahead(value, step):
        return lax.ppermute(value, "tensor", [(s, (s - step) % parts) for s in range(parts)])

    def tensor_swap(value, distance):
        return lax.ppermute(value, "tensor", [(s, s ^ distance) for s in range(parts)])

    def dp_swap(value, distance):
        return lax.ppermute(value, "dp", [(s, s ^ distance) for s in range(dp_count)])

    steps = sorted(range(1, parts), key=lambda k: (-min(k, parts - k), k))

    def exchange(blocks):
        return lax.all_to_all(blocks, "tensor", 0, 0, tiled=True)

    levels = []
    left = dp_count
    stride = 1
    while left > 1:
        radix = 2 if (left % 4 or left == dp_count) and left % 2 == 0 else 4
        levels.append((stride, radix))
        stride *= radix
        left //= radix

    high = width // dp_count
    fast = [radix for _, radix in levels[:2]] == [2, dp_count // 2] and high % 16 == 0
    halves = (dp_count // 2, high) if fast else None
    dp_digit = dp_me % 2

    radix = dp_count // 2

    def dp_first(made, earlier=(), cut=0):
        if fast:
            keep, *send = made
            got = [dp_swap(one, 1) for one in send]
            return level_sum((dp_me // 2).reshape(1), keep, got, earlier, cut)
        return (dp_level(made[0].reshape(dp_count, high, -1), levels[0], dp_count),)

    def dp_level(current, level, remaining):
        stride, radix = level
        digit = (dp_me // stride) % radix
        view = current.reshape((remaining // radix, radix) + current.shape[1:])
        total = lax.dynamic_index_in_dim(view, digit, 1, False).astype(F32)
        for m in sorted(range(1, radix), reverse=True):
            piece = lax.dynamic_index_in_dim(view, digit ^ m, 1, False).astype(LOW)
            total = total + dp_swap(piece, m * stride).astype(F32)
        return total

    def dp_send(blocks):
        return [dp_swap(one, 2 * m) for m, one in enumerate(blocks, 1)]

    def dp_slow(blocks):
        (current,) = blocks
        for level in levels[1:]:
            current = dp_level(current, level, current.shape[0])
        return current[0]

    def dp_gather_first(value):
        stride, radix = levels[0]
        joined = value[None]
        return jnp.concatenate([joined] + [dp_swap(joined, m * stride) for m in range(1, radix)])

    def dp_gather_rest(joined):
        current = [joined]
        for stride, radix in levels[1:]:
            joined = current[0] if len(current) == 1 else jnp.concatenate(current)
            current = [joined] + [dp_swap(joined, m * stride) for m in range(1, radix)]
        return current

    def pair_sum(values_in):
        while values_in.shape[0] > 1:
            values_in = values_in[0::2] + values_in[1::2]
        return values_in[0]

    barrier = lax.optimization_barrier
    me_ref = me.reshape(1)
    cond_act, silu_back = jax.vjp(jax.nn.silu, conditioning.astype(F32))
    cond_low = cond_act.astype(LOW).reshape(cond_count, width)
    mod_part = (
        jnp.dot(cond_low, w_ada, preferred_element_type=F32) + b_ada.astype(F32)
    ).astype(LOW)
    mod_all = exchange(jnp.broadcast_to(mod_part[None], (parts,) + mod_part.shape))
    modulation = mod_all.transpose(1, 0, 2).reshape(cond_count, -1)
    modulation = jnp.pad(modulation, ((0, HOT - cond_count), (0, 0)))

    rows = 4 * local_width // PIECES
    slot = dp_me % PIECES
    qkv_rows = w_qkv.transpose(1, 2, 0).reshape(3 * local_width, width)
    out_rows = w_out.T
    start = slot * rows
    piece = jnp.where(
        start < 3 * local_width,
        lax.dynamic_slice_in_dim(
            qkv_rows, jnp.minimum(start, 3 * local_width - rows), rows, 0
        ),
        lax.dynamic_slice_in_dim(out_rows, jnp.maximum(start - 3 * local_width, 0), rows, 0),
    )
    table = slot ^ jnp.array(
        [2 * a + c for c in (0, 1) for a in range(PIECES // 2)], jnp.int32
    )
    in_order = jnp.arange(PIECES, dtype=jnp.int32)
    order = [1] + list(range(parts - 1, 1, -1))
    pairs = [
        (qkv_rows.reshape(-1, rows, width), out_rows.reshape(-1, rows, width), 0)
    ] + [None] * (parts - 1)
    arrived = from_ahead(piece, order[0])

    seg_col = segments.reshape(length, 1)
    crop_match = seg_col == jnp.arange(crop_count, dtype=jnp.int32)[None, :]
    token_cond = jnp.sum(jnp.where(crop_match, crop_cond.reshape(1, crop_count), 0), -1)
    hot = (token_cond[:, None] == jnp.arange(HOT, dtype=jnp.int32)[None, :]).astype(LOW)
    hot_rows = (token_cond[None, :] == jnp.arange(HOT, dtype=jnp.int32)[:, None]).astype(LOW)

    def per_token(index, chosen):
        return jnp.dot(
            chosen,
            modulation[:, index * width : (index + 1) * width],
            preferred_element_type=F32,
        )

    def pass_on(block):
        return [block, dp_swap(block, 2), dp_swap(block, 4)]

    def relay(passed):
        block, beside, above = passed
        cut = block.shape[0] // 2 // 16 * 16
        return passed + [dp_swap(above[:cut], 2), dp_swap(beside[cut:], 4)]

    def finish(passed):
        near = jnp.stack(passed[:3] + [jnp.concatenate(passed[3:])])
        return (near, dp_swap(near, 1))

    second_z = from_ahead(piece, order[1])
    modulation, arrived, second_z, piece = barrier((modulation, arrived, second_z, piece))
    nearest = jnp.concatenate([arrived, second_z])
    passed = pass_on(nearest)
    last_z = from_ahead(piece, order[2])
    resid_in = tokens.astype(F32)
    normed_attn, _ = normalize_rows(resid_in)
    first_in = (normed_attn * (1.0 + per_token(1, hot)) + per_token(0, hot)).astype(LOW)
    saved = [None] * parts
    attended = [None] * parts
    w_outs = [None] * parts

    def group(k, chosen_table):
        saved[k], attended[k], w_outs[k] = attend_group(
            chosen_table, first_in, seg_col, segments, pairs[k], local_width
        )

    group(0, in_order)
    attended[0], passed, last_z, grad_in = barrier((attended[0], passed, last_z, d_out))
    passed = relay(passed)
    last = pass_on(last_z)
    d_mixed = (grad_in.astype(F32) * per_token(5, hot)).astype(LOW)
    d_b_down = jnp.sum(d_mixed.astype(F32), 0)
    d_hidden = jnp.dot(d_mixed, w_down, preferred_element_type=F32)
    d_hidden, passed = barrier((d_hidden, passed))
    both = finish(passed)
    pairs[order[0]], pairs[order[1]] = both + (0,), both + (1,)
    group(order[0], table)
    attended[order[0]], last = barrier((attended[order[0]], last))
    last = relay(last)
    group(order[1], table)
    attended[order[1]], last = barrier((attended[order[1]], last))
    pairs[order[2]] = finish(last) + (0,)
    group(order[2], table)
    branch, middle, second_in, hidden, d_pre, d_second_parts, d_b_up = mlp_forward(
        me_ref,
        attended,
        w_outs,
        b_out.astype(F32).reshape(1, width),
        tokens,
        hot,
        modulation,
        d_hidden,
        w_up,
        b_up.astype(F32).reshape(1, -1),
    )
    second_arrived = exchange(d_second_parts)

    mlp_low, gate_sums = mlp_down(hidden, w_down, d_out, hot_rows, parts)
    digit_ref = dp_digit.reshape(1)
    mlp_made = mlp_grads(digit_ref, d_mixed, hidden, second_in, d_pre, halves)
    units = w_down.shape[1]
    mlp_blocks = dp_first(mlp_made, cut=units)
    second_arrived, mlp_blocks, mlp_low, gate_sums = barrier(
        (second_arrived, mlp_blocks, mlp_low, gate_sums)
    )
    spread, d_second, d_middle_own = turn_back(
        me_ref, second_arrived, modulation, middle, d_out, hot
    )
    d_middle = exchange(spread).reshape(length, width)

    half_type = shaped((high, units), F32)
    if fast:
        down_got = dp_send(mlp_blocks[1:radix])
        (d_w_down,) = finish_sum([(mlp_blocks[0], 0, units)], down_got, [half_type])
    else:
        d_w_down, d_w_up = finish_sum([(dp_slow(mlp_blocks), 0, 2 * units)], [], [half_type] * 2)
    d_middle, d_w_down, mlp_low = barrier((d_middle, d_w_down, mlp_low))
    mlp_arrived = exchange(mlp_low)
    d_branch, d_local, d_near, *attention_parts, d_b_out = back_first(
        digit_ref,
        d_middle,
        hot,
        modulation,
        seg_col,
        segments,
        out_rows,
        saved[0],
        first_in,
        attended[0],
        w_outs[1],
        saved[1],
        halves,
    )
    attention_blocks = dp_first(attention_parts, mlp_blocks[radix:])
    d_branch, mlp_arrived, attention_blocks, d_second = barrier(
        (d_branch, mlp_arrived, attention_blocks, d_second)
    )
    output_parts = output_rows(
        me_ref,
        mlp_arrived,
        b_down.astype(F32).reshape(1, width),
        middle,
        modulation,
        hot,
        branch,
        d_second,
        d_middle_own,
        d_out,
        hot_rows,
        gate_sums,
        cond_count,
    )
    output_arrived = exchange(output_parts)
    d_branch, output_parts, attention_blocks = barrier((d_branch, output_parts, attention_blocks))
    rest_got = dp_send(attention_blocks[1:]) if fast else [dp_slow(attention_blocks)]
    d_tokens, attn_sums = back_remote(
        me_ref,
        table,
        d_branch,
        seg_col,
        segments,
        d_local,
        d_near,
        qkv_rows,
        hot,
        hot_rows,
        modulation,
        tokens,
        d_middle,
        pairs[1:],
        saved[1:],
    )
    attn_sums, output_arrived, rest_got = barrier(
        (attn_sums, output_arrived, rest_got)
    )
    mod_width = w_ada.shape[1]

    def row(values_in):
        flat = values_in.reshape(-1, values_in.shape[-1]).astype(F32)
        return jnp.pad(flat, ((0, 0), (0, mod_width - flat.shape[1])))

    others = jnp.concatenate(
        [jnp.zeros((cond_count, mod_width), F32)]
        + [row(one) for one in (cond_low, d_b_out, d_b_up, d_b_down[None])]
        + [jnp.zeros((5, mod_width), F32)]
    )
    packed, output = mod_gradient(me_ref, attn_sums, output_arrived, others, cond_count)
    joined = dp_gather_first(packed)
    gathered = dp_gather_rest(joined)
    d_silu_part = mod_product(joined, w_ada.T)
    attention_types = [shaped((3, high, local_width), F32), shaped((high, local_width), F32)]
    if fast:
        d_w_up, d_w_qkv, d_w_out = finish_sum(
            [(mlp_blocks[0], units, units), (attention_blocks[0], 0, 4 * local_width)],
            rest_got,
            [half_type, *attention_types],
        )
    else:
        d_w_qkv, d_w_out = finish_sum(
            [(rest_got[0], 0, 4 * local_width)], [], attention_types
        )
    d_w_qkv = d_w_qkv.transpose(1, 0, 2)
    d_silu = pair_sum(
        jnp.stack([d_silu_part] + [tensor_swap(d_silu_part, m) for m in range(1, parts)])
    )[:cond_count]
    d_conditioning = silu_back(d_silu.reshape(conditioning.shape))[0]
    d_w_ada, d_b_ada, d_b_out, d_b_up, d_b_down = factors(
        dp_me.reshape(1), gathered, width // dp_count, d_b_up.shape[1], width, cond_count
    )
    return (
        output,
        d_tokens,
        d_conditioning,
        d_w_ada,
        d_b_ada,
        d_w_qkv,
        d_w_out,
        d_b_out,
        d_w_up,
        d_b_up,
        d_w_down,
        d_b_down,
    )


def solution(mesh):
    return jax.shard_map(
        shards,
        mesh=mesh,
        in_specs=(
            P("dp", None),
            P("dp", None, None),
            P("dp", None),
            P("dp", None),
            P(None, "tensor"),
            P("tensor"),
            P(None, None, "tensor"),
            P(None, "tensor"),
            P(),
            P(None, "tensor"),
            P("tensor"),
            P(None, "tensor"),
            P(),
            P("dp", None),
        ),
        out_specs=(
            P("dp", None),
            P("dp", None),
            P("dp", None, None),
            P("dp", "tensor"),
            P("tensor"),
            P("dp", None, "tensor"),
            P("dp", "tensor"),
            P(),
            P("dp", "tensor"),
            P("tensor"),
            P("dp", "tensor"),
            P(),
        ),
        check_vma=False,
    )
```

```python
import jax
import jax.numpy as jnp
from jax import lax
from jax.experimental import pallas as pl
from jax.experimental.pallas import tpu as pltpu
from jax.sharding import PartitionSpec as P

HD = 72
F32 = jnp.float32
LOW = jnp.bfloat16
NEG = -1e30
LOG2E = 1.4426950408889634
PIECES = 8
HOT = 8
SMEM = pl.BlockSpec(memory_space=pltpu.SMEM)
HBM = pl.BlockSpec(memory_space=pltpu.HBM)
SMALL = pl.CostEstimate(flops=1 << 20, transcendentals=0, bytes_accessed=1 << 20)


def dot_nn(a, b):
    return lax.dot_general(a, b, (((1,), (0,)), ((), ())), preferred_element_type=F32)


def dot_nt(a, b):
    return lax.dot_general(a, b, (((1,), (1,)), ((), ())), preferred_element_type=F32)


def dot_tn(a, b):
    return lax.dot_general(a, b, (((0,), (0,)), ((), ())), preferred_element_type=F32)


def normalize_rows(values):
    average = jnp.mean(values, -1, keepdims=True)
    centered = values - average
    variance = jnp.mean(centered * centered, -1, keepdims=True)
    inverse = lax.rsqrt(variance + 1e-06)
    return (centered * inverse, inverse)


def normalize_back(gradient, normed, inverse):
    return inverse * (
        gradient
        - jnp.mean(gradient, -1, keepdims=True)
        - normed * jnp.mean(gradient * normed, -1, keepdims=True)
    )


def softmax_rows(queries, key_vecs, bias):
    scaled = dot_nt(queries, key_vecs) * (HD**-0.5 * LOG2E) + bias
    exponent = jnp.exp2(scaled - jnp.max(scaled, -1, keepdims=True))
    return exponent * (1.0 / jnp.sum(exponent, -1, keepdims=True))


def piece_copies(table, pair, into, sems):
    first, second, step, rows = pair
    ahead = first.shape[0]
    copies = []
    for n in range(PIECES):
        source = first.at[n] if n < ahead else second.at[n - ahead]
        source = source.at[step * rows : (step + 1) * rows, :]
        place = pl.ds(pl.multiple_of(table[n] * rows, 16), rows)
        copies.append(pltpu.make_async_copy(source, into.at[place, :], sems.at[n]))
    return copies


class Staged:
    def __init__(self, sources, ins, in_sems, outs, targets, out_sems):
        self.coming = [
            pltpu.make_async_copy(a, b, in_sems.at[n])
            for n, (a, b) in enumerate(zip(sources, ins))
        ]
        self.going = [[] for _ in outs]
        self.ins, self.outs = ins, outs
        self.here = set()
        self.pairs, self.out_sems = list(zip(outs, targets)), out_sems
        for one in self.coming:
            one.start()

    def get(self, n):
        if n not in self.here:
            self.here.add(n)
            self.coming[n].wait()
        return self.ins[n]

    def put(self, n):
        one = pltpu.make_async_copy(*self.pairs[n], self.out_sems.at[n])
        one.start()
        self.going[n].append(one)

    def put_part(self, n, part, parts, size):
        source, target = self.pairs[n]
        place = slice(part * size, (part + 1) * size)
        one = pltpu.make_async_copy(
            source.at[place], target.at[place], self.out_sems.at[len(self.pairs) * (1 + part) + n]
        )
        one.start()
        self.going[n].append(one)

    def finish(self):
        for n in range(len(self.coming)):
            self.get(n)
        for n, made in enumerate(self.going):
            if not made:
                self.put(n)
        for made in self.going:
            for one in made:
                one.wait()


OWN_ROWS = "rows"
OWN_FREE = "rows anywhere"
FREE = "anywhere"
OWN_COLUMNS = "columns"


def staged_call(
    body, scalars, ins, outs, name, mib, raw=(), raw_outs=(), scratch=(), small=True, share=0
):
    plain = [one if isinstance(one, tuple) else (one, None) for one in ins]
    arrays = [
        one if kind in (FREE, OWN_FREE) else pltpu.with_memory_space_constraint(one, pltpu.HBM)
        for one, kind in plain
    ]
    shapes = []
    for one, kind in plain:
        shape = list(one.shape)
        if kind in (OWN_ROWS, OWN_FREE):
            shape[0] = share
        if kind == OWN_COLUMNS:
            shape[1] = share
        shapes.append(pltpu.VMEM(tuple(shape), one.dtype))
    counts = [
        len(scalars),
        len(ins),
        len(raw),
        len(outs),
        len(raw_outs),
        len(ins),
        len(outs),
    ]

    def kernel(*refs):
        groups, at = [], 0
        for count in counts:
            groups.append(refs[at : at + count])
            at += count
        scalar_refs, sources, raw_refs, targets, raw_targets, in_refs, out_refs = groups
        in_sems, out_sems = refs[at : at + 2]
        picked = []
        for source, (_, kind) in zip(sources, plain):
            if kind in (OWN_ROWS, OWN_FREE):
                source = source.at[pl.ds(pl.multiple_of(scalar_refs[0][0] * share, 16), share), :]
            if kind == OWN_COLUMNS:
                source = source.at[:, pl.ds(pl.multiple_of(scalar_refs[0][0] * share, 128), share)]
            picked.append(source)
        staged = Staged(picked, in_refs, in_sems, out_refs, targets, out_sems)
        body(scalar_refs, staged, raw_refs + raw_targets, refs[at + 2 :])
        staged.finish()

    return pl.pallas_call(
        kernel,
        out_shape=tuple(pltpu.HBM(one.shape, one.dtype) for one in (*outs, *raw_outs)),
        in_specs=[SMEM] * len(scalars) + [HBM] * (len(ins) + len(raw)),
        out_specs=(HBM,) * (len(outs) + len(raw_outs)),
        scratch_shapes=shapes
        + [pltpu.VMEM(one.shape, one.dtype) for one in outs]
        + [pltpu.SemaphoreType.DMA((len(ins),)), pltpu.SemaphoreType.DMA((3 * max(len(outs), 1),))]
        + list(scratch),
        compiler_params=pltpu.CompilerParams(vmem_limit_bytes=mib << 20),
        cost_estimate=SMALL if small else None,
        name=name,
    )(*scalars, *arrays, *raw)


def shaped(shape, dtype):
    return jax.ShapeDtypeStruct(shape, dtype)


def modulate(hot, modulation, index):
    model = modulation.shape[1] // 6
    return dot_nn(hot[...], modulation[:, index * model : (index + 1) * model])


def fill_bias(bias, seg_col, seg_row):
    bias[...] = jnp.where(seg_col[...] == seg_row[...], 0.0, NEG)


def attend_group(table, first_in, seg_col, seg_row, pair, width):
    length, model = first_in.shape
    total = 4 * width

    def body(scalars, staged, raw, scratch):
        weights, bias, sems = scratch
        pieces = piece_copies(scalars[0], (*raw, pair[2], total // PIECES), weights, sems)
        for c in pieces:
            c.start()
        fill_bias(bias, staged.get(1), staged.get(2))
        projected, attended, w_out = staged.outs
        for c in pieces:
            c.wait()
        projected[...] = dot_nt(staged.get(0)[...], weights[: 3 * width]).astype(LOW)
        staged.put(0)
        w_out[...] = weights[3 * width :]
        staged.put(2)
        for h in range(width // HD):
            queries, key_vecs, values = [
                projected[:, j * width + h * HD : j * width + (h + 1) * HD] for j in range(3)
            ]
            probs = softmax_rows(queries, key_vecs, bias[...])
            attended[:, h * HD : (h + 1) * HD] = dot_nn(probs.astype(LOW), values).astype(LOW)

    return staged_call(
        body,
        [table],
        [(first_in, FREE), (seg_col, FREE), (seg_row, FREE)],
        [
            shaped((length, 3 * width), LOW),
            shaped((length, width), LOW),
            shaped((width, model), LOW),
        ],
        "attend_group",
        32,
        raw=pair[:2],
        scratch=[
            pltpu.VMEM((total, model), LOW),
            pltpu.VMEM((length, length), F32),
            pltpu.SemaphoreType.DMA((PIECES,)),
        ],
    )


def head_gradients(qkv, d_attended, bias, low_probs, d_scores, d_projected):
    width = d_attended.shape[1]
    scale = HD**-0.5
    for h in range(width // HD):
        columns = slice(h * HD, (h + 1) * HD)
        queries, key_vecs, values = [
            qkv[:, j * width + h * HD : j * width + (h + 1) * HD] for j in range(3)
        ]
        d_head = d_attended[:, columns]
        probs = softmax_rows(queries, key_vecs, bias[...])
        d_probs = dot_nt(d_head, values)
        inner = jnp.sum(d_probs * probs, -1, keepdims=True)
        low_probs[h] = probs.astype(LOW)
        d_scores[h] = (probs * (d_probs - inner)).astype(LOW)
        d_projected[:, h * HD : (h + 1) * HD] = (dot_nn(d_scores[h], key_vecs) * scale).astype(
            LOW
        )
        d_projected[:, width + h * HD : width + (h + 1) * HD] = (
            dot_tn(d_scores[h], queries) * scale
        ).astype(LOW)
        d_projected[:, 2 * width + h * HD : 2 * width + (h + 1) * HD] = dot_tn(
            low_probs[h], d_head
        ).astype(LOW)


def split_sum(hot_rows, values_in):
    high = values_in.astype(LOW)
    rest = values_in - high.astype(F32)
    mid = rest.astype(LOW)
    low = (rest - mid.astype(F32)).astype(LOW)
    return dot_nn(hot_rows, high) + dot_nn(hot_rows, mid) + dot_nn(hot_rows, low)


def mlp_forward(me, attended, w_out, b_out, tokens, hot, modulation, d_hidden, w_up, b_up):
    parts = len(attended)
    length, model = tokens.shape
    units = w_up.shape[1]
    share = length // parts

    def body(scalars, staged, raw, scratch):
        held = scratch[0]
        own_branch, own_middle, second_in, hidden, d_pre, d_second, d_b_up = staged.outs
        rows = length // 2
        sums = jnp.zeros((1, units), F32)
        for step in range(2):
            block = slice(step * rows, (step + 1) * rows)
            branch = staged.get(2 * parts)[...]
            for k in range(parts):
                branch = branch + dot_nn(staged.get(k)[block], staged.get(parts + k)[...])
            chosen, table = staged.get(2 * parts + 2)[block], staged.get(2 * parts + 3)
            stream = staged.get(2 * parts + 1)[block].astype(F32) + (
                modulate(chosen, table, 2) * branch
            )
            held[0, block] = branch
            held[1, block] = stream
            normed, _ = normalize_rows(stream)
            second = (normed * (1.0 + modulate(chosen, table, 4)) + modulate(chosen, table, 3)).astype(LOW)
            second_in[block] = second
            staged.put_part(2, step, 2, rows)
            weights = staged.get(2 * parts + 5)
            u = dot_nn(second, weights[...]) + staged.get(2 * parts + 6)[...]
            root = 0.7978845608028654
            square = u * u
            bent = jnp.tanh(root * u * (1.0 + 0.044715 * square))
            half = 0.5 * (1.0 + bent)
            hidden[block] = (u * half).astype(LOW)
            staged.put_part(3, step, 2, rows)
            slope = half + 0.5 * u * (1.0 - bent * bent) * (root * (1.0 + 3 * 0.044715 * square))
            low = (staged.get(2 * parts + 4)[block] * slope).astype(LOW)
            d_pre[block] = low
            staged.put_part(4, step, 2, rows)
            sums = sums + jnp.sum(low.astype(F32), 0, keepdims=True)
            added = dot_nt(low, weights[...]).astype(LOW)
            for n in range(rows // share):
                d_second[step * (rows // share) + n] = added[n * share : (n + 1) * share]
            staged.put_part(5, step, 2, rows // share)
        d_b_up[...] = sums
        mine = pl.ds(pl.multiple_of(scalars[0][0] * share, 8), share)
        own_branch[...] = held[0, mine, :]
        own_middle[...] = held[1, mine, :]

    return staged_call(
        body,
        [me],
        [*attended, *w_out, (b_out, FREE), tokens, (hot, FREE), (modulation, FREE), (d_hidden, FREE), w_up, (b_up, FREE)],
        [
            shaped((share, model), F32),
            shaped((share, model), F32),
            shaped((length, model), LOW),
            shaped((length, units), LOW),
            shaped((length, units), LOW),
            shaped((parts, share, model), LOW),
            shaped((1, units), F32),
        ],
        "mlp_forward",
        48,
        scratch=[pltpu.VMEM((2, length, model), F32)],
        small=False,
    )


def mlp_down(hidden, w_down, d_out, hot_rows, parts):
    length, model = d_out.shape
    share = length // parts
    count = hot_rows.shape[0]

    def body(scalars, staged, raw, scratch):
        low, sums = staged.outs
        total = jnp.zeros((count, model), F32)
        rows = length // 2
        for step in range(2):
            block = slice(step * rows, (step + 1) * rows)
            added = dot_nt(staged.get(0)[block], staged.get(1)[...])
            for n in range(rows // share):
                low[step * (rows // share) + n] = added[n * share : (n + 1) * share].astype(LOW)
            staged.put_part(0, step, 2, rows // share)
            total = total + split_sum(
                staged.get(3)[:, block], staged.get(2)[block].astype(F32) * added
            )
        sums[...] = total

    return staged_call(
        body,
        [],
        [hidden, w_down, d_out, (hot_rows, FREE)],
        [shaped((parts, share, model), LOW), shaped((count, model), F32)],
        "mlp_down",
        32,
    )


def hand_out_types(halves, rows, columns):
    if halves is None:
        return [shaped((rows, columns), F32)]
    count, high = halves
    return [shaped((count, high, columns), F32)] + [shaped((high, columns), LOW)] * count


def hand_out(digit, whole, outs):
    if len(outs) == 1:
        outs[0][...] = whole[...]
        return
    keep, *send = outs
    high = keep.shape[1]
    for n, one in enumerate(send):
        keep[n] = whole[pl.ds(pl.multiple_of((2 * n + digit) * high, 8), high), :]
        one[...] = whole[pl.ds(pl.multiple_of((2 * n + 1 - digit) * high, 8), high), :].astype(LOW)


def mlp_grads(digit, d_mixed, hidden, second_in, d_pre, halves):
    model, units = d_mixed.shape[1], hidden.shape[1]

    def body(scalars, staged, raw, scratch):
        whole = scratch[0]
        whole[:, :units] = dot_tn(staged.get(0)[...], staged.get(1)[...])
        whole[:, units:] = dot_tn(staged.get(2)[...], staged.get(3)[...])
        hand_out(scalars[0][0], whole, staged.outs)

    return staged_call(
        body,
        [digit],
        [(d_mixed, FREE), hidden, second_in, d_pre],
        hand_out_types(halves, model, 2 * units),
        "mlp_grads",
        48,
        scratch=[pltpu.VMEM((model, 2 * units), F32)],
    )


def level_sum(digit, keep, got, earlier=(), cut=0):
    radix, rows, columns = keep.shape
    before = earlier[0].shape[1] if earlier else 0
    widths = [cut, columns - cut] if cut else [before + columns]

    def body(scalars, staged, raw, scratch):
        came = scratch[0]
        mine = scalars[0][0]
        for n in range(radix):
            came[n] = staged.get(1 + n)[...]
        kept = staged.get(0)
        for m in range(1, radix):
            other = jnp.bitwise_xor(mine, m)
            total = (kept[other] + came[other].astype(F32)).astype(LOW)
            if cut:
                staged.outs[m][...] = total[:, :cut]
                staged.outs[radix - 1 + m][...] = total[:, cut:]
                staged.put(radix - 1 + m)
            else:
                if earlier:
                    staged.outs[m][:, :before] = staged.get(radix + m)[...]
                staged.outs[m][:, before:] = total
            staged.put(m)
        staged.outs[0][...] = kept[mine] + came[mine].astype(F32)

    return staged_call(
        body,
        [digit],
        [keep, *[(one, FREE) for one in got], *earlier],
        [shaped((rows, columns), F32)]
        + [shaped((rows, wide), LOW) for wide in widths for _ in range(radix - 1)],
        "level_sum",
        40,
        scratch=[pltpu.VMEM(keep.shape, LOW)],
    )


def finish_sum(owns, got, types):
    def body(scalars, staged, raw, scratch):
        n, at, base, total = 0, 0, 0, None
        for out in staged.outs:
            width = out.shape[-1]
            for j in range(out.shape[0] if len(out.shape) == 3 else 1):
                if total is None:
                    _, begin, wide = owns[n]
                    total = staged.get(n)[:, begin : begin + wide]
                    for k in range(len(got)):
                        total = total + staged.get(len(owns) + k)[:, base : base + wide].astype(F32)
                target = out.at[j] if len(out.shape) == 3 else out
                target[...] = total[:, at : at + width]
                at += width
                if at == wide:
                    n, at, base, total = n + 1, 0, base + wide, None

    return staged_call(
        body, [], [*[one[0] for one in owns], *[(one, FREE) for one in got]], types, "finish_sum", 32
    )


def turn_back(me, arrived, modulation, middle, d_out, hot):
    parts, share, model = arrived.shape

    def body(scalars, staged, raw, scratch):
        spread, d_second, d_middle = staged.outs
        normed, inverse = normalize_rows(staged.get(2)[...])
        scale = modulate(staged.get(4), staged.get(1), 4)
        came = staged.get(0)
        grad = came[0].astype(F32)
        for k in range(1, parts):
            grad = grad + came[k].astype(F32)
        d_second[...] = grad
        moved = staged.get(3)[...].astype(F32) + normalize_back(
            grad * (1.0 + scale), normed, inverse
        )
        d_middle[...] = moved
        for k in range(parts):
            spread[k] = moved.astype(LOW)

    return staged_call(
        body,
        [me],
        [(arrived, FREE), (modulation, FREE), middle, (d_out, OWN_ROWS), (hot, OWN_FREE)],
        [
            shaped(arrived.shape, LOW),
            shaped((share, model), F32),
            shaped((share, model), F32),
        ],
        "turn_back",
        16,
        share=share,
    )


def own_sums(me, branch, middle, d_second, d_middle, d_out, b_down, hot_rows, gate_sums, conds):
    share, model = middle.shape
    extra = 4 * conds

    def body(scalars, staged, raw, scratch):
        held = scratch[0]
        normed, _ = normalize_rows(staged.get(1)[...])
        second, moved = staged.get(2), staged.get(3)
        each = [
            moved[...] * staged.get(0)[...],
            second[...],
            second[...] * normed,
            staged.get(4)[...].astype(F32) * staged.get(5)[...],
        ]
        for n, one in enumerate(each):
            added = split_sum(staged.get(6)[...], one)
            if n == len(each) - 1:
                added = added + staged.get(7)[...]
            held[n * conds : (n + 1) * conds] = added[:conds]
        high = held[...].astype(LOW)
        staged.outs[0][:extra] = high
        staged.outs[0][extra:] = (held[...] - high.astype(F32)).astype(LOW)

    return staged_call(
        body,
        [me],
        [
            branch,
            middle,
            d_second,
            d_middle,
            (d_out, OWN_ROWS),
            (b_down, FREE),
            (hot_rows, OWN_COLUMNS),
            (gate_sums, FREE),
        ],
        [shaped((2 * extra, model), LOW)],
        "own_sums",
        24,
        scratch=[pltpu.VMEM((extra, model), F32)],
        share=share,
    )[0]


def output_rows(me, arrived, b_down, middle, modulation, hot, sums):
    parts, share, model = arrived.shape
    below = sums.shape[0]

    def body(scalars, staged, raw, scratch):
        came = staged.get(0)
        total = staged.get(1)[...]
        for k in range(parts):
            total = total + came[k].astype(F32)
        made = staged.get(2)[...] + modulate(staged.get(4), staged.get(3), 5) * total
        low = made.astype(LOW)
        spread = staged.outs[0]
        for k in range(parts):
            spread[k, :share] = low
            spread[k, share:] = staged.get(5)[...]

    return staged_call(
        body,
        [me],
        [
            (arrived, FREE),
            (b_down, FREE),
            middle,
            (modulation, FREE),
            (hot, OWN_FREE),
            sums,
        ],
        [shaped((parts, share + below, model), LOW)],
        "output_rows",
        24,
        share=share,
    )[0]


def back_scratch(length, width):
    heads = width // HD
    return [
        pltpu.VMEM((length, width), LOW),
        pltpu.VMEM((heads, length, length), LOW),
        pltpu.VMEM((heads, length, length), LOW),
        pltpu.VMEM((length, length), F32),
    ]


def back_first(
    digit,
    d_middle,
    hot,
    modulation,
    seg_col,
    seg_row,
    w_out,
    qkv,
    first_in,
    attended,
    near_out,
    near_qkv,
    halves,
):
    length, model = d_middle.shape
    width = attended.shape[1]

    def body(scalars, staged, raw, scratch):
        (
            d_attended,
            low_probs,
            d_scores,
            bias,
            weights,
            projected,
            d_projected,
            whole,
            sems,
        ) = scratch
        fetches = [
            pltpu.make_async_copy(raw[n], weights.at[n, 3 * width :, :], sems.at[n])
            for n in range(2)
        ] + [pltpu.make_async_copy(raw[2 + n], projected.at[n], sems.at[2 + n]) for n in range(2)]
        for c in fetches:
            c.start()
        d_branch, d_local, d_near, *outs, d_b_out = staged.outs
        gate = modulate(staged.get(1), staged.get(2), 2)
        d_branch[...] = (staged.get(0)[...].astype(F32) * gate).astype(LOW)
        staged.put(0)
        d_b_out[...] = jnp.sum(d_branch[...].astype(F32), 0, keepdims=True)
        fill_bias(bias, staged.get(3), staged.get(4))
        for c in fetches:
            c.wait()

        def group_step(group, carry):
            slot = lax.rem(group, 2)
            used = weights.at[slot]
            d_attended[...] = dot_nt(d_branch[...], used[3 * width :]).astype(LOW)
            head_gradients(
                projected.at[slot], d_attended, bias, low_probs, d_scores, d_projected
            )

            @pl.when(group == 0)
            def _():
                d_local[...] = d_projected[...]

            @pl.when(group == 1)
            def _():
                d_near[...] = d_projected[...]

            return carry

        lax.fori_loop(0, 2, group_step, 0)
        staged.put(1)
        staged.put(2)
        whole[:, : 3 * width] = dot_tn(staged.get(5)[...], d_local[...])
        whole[:, 3 * width :] = dot_tn(d_branch[...], staged.get(6)[...])
        hand_out(scalars[0][0], whole, outs)

    return staged_call(
        body,
        [digit],
        [
            (d_middle, FREE),
            (hot, FREE),
            (modulation, FREE),
            (seg_col, FREE),
            (seg_row, FREE),
            (first_in, FREE),
            attended,
        ],
        [
            shaped((length, model), LOW),
            shaped((length, 3 * width), LOW),
            shaped((length, 3 * width), LOW),
            *hand_out_types(halves, model, 4 * width),
            shaped((1, model), F32),
        ],
        "back_first",
        52,
        raw=[w_out, near_out, qkv, near_qkv],
        scratch=back_scratch(length, width)
        + [
            pltpu.VMEM((2, 4 * width, model), LOW),
            pltpu.VMEM((2, length, 3 * width), LOW),
            pltpu.VMEM((length, 3 * width), LOW),
            pltpu.VMEM((model, 4 * width), F32),
            pltpu.SemaphoreType.DMA((4,)),
        ],
    )


def back_remote(
    me,
    table,
    d_branch,
    seg_col,
    seg_row,
    d_local,
    d_near,
    w_qkv,
    hot,
    hot_rows,
    modulation,
    tokens,
    d_middle,
    pairs,
    saved,
):
    length, model = d_branch.shape
    width = d_local.shape[1] // 3
    remote = len(saved)
    parts = remote + 1
    rows = 4 * width // PIECES

    def body(scalars, staged, raw, scratch):
        (
            d_attended,
            low_probs,
            d_scores,
            bias,
            weights,
            projected,
            d_projected,
            d_first,
            sems,
            saved_sems,
        ) = scratch
        me_ref, table_ref = scalars
        pieces, qkvs = raw[: 2 * remote], raw[2 * remote :]
        d_tokens, sums = staged.outs

        def copies(k, slot):
            pair = (pieces[2 * k - 2], pieces[2 * k - 1], pairs[k - 1][2], rows)
            return piece_copies(table_ref, pair, weights.at[slot], sems.at[slot]) + [
                pltpu.make_async_copy(qkvs[k - 1], projected.at[slot], saved_sems.at[slot])
            ]

        def ahead_of(group):
            return lax.rem(group - me_ref[0] + parts, parts)

        def fetch(group, slot):
            for k in range(1, parts):

                @pl.when(ahead_of(group) == k)
                def _():
                    for c in copies(k, slot):
                        c.start()

        fetch(0, 0)
        d_first[...] = jnp.zeros_like(d_first)
        fill_bias(bias, staged.get(1), staged.get(2))
        branch_grad, own_grad, near_grad, own_weights = [staged.get(n) for n in (0, 3, 4, 5)]

        def group_step(group, carry):
            slot = lax.rem(group, 2)

            @pl.when(group < parts - 1)
            def _():
                fetch(group + 1, 1 - slot)

            used = weights.at[slot]

            @pl.when(ahead_of(group) == 0)
            def _():
                d_projected[...] = own_grad[...]
                used[: 3 * width] = own_weights[...]

            @pl.when(ahead_of(group) != 0)
            def _():
                for c in copies(1, slot):
                    c.wait()

            @pl.when(ahead_of(group) == 1)
            def _():
                d_projected[...] = near_grad[...]

            @pl.when(ahead_of(group) > 1)
            def _():
                d_attended[...] = dot_nt(branch_grad[...], used[3 * width :]).astype(LOW)
                head_gradients(
                    projected.at[slot], d_attended, bias, low_probs, d_scores, d_projected
                )

            d_first[...] += dot_nn(d_projected[...], used[: 3 * width])
            return carry

        lax.fori_loop(0, parts, group_step, 0)
        total = jnp.zeros(sums.shape, F32)
        step = length // 4
        chosen, turned, modulation_ref, tokens_ref, middle_ref = [
            staged.get(n) for n in (6, 7, 8, 9, 10)
        ]
        for r in range(4):
            block = slice(r * step, (r + 1) * step)
            normed, inverse = normalize_rows(tokens_ref[block].astype(F32))
            scale = modulate(chosen[block], modulation_ref, 1)
            grad = d_first[block]
            d_tokens[block] = middle_ref[block].astype(F32) + normalize_back(
                grad * (1.0 + scale), normed, inverse
            )
            total = total + jnp.concatenate(
                [split_sum(turned[:, block], v) for v in (grad, grad * normed)], 1
            )
        sums[...] = total

    return staged_call(
        body,
        [me, table],
        [
            d_branch,
            (seg_col, FREE),
            (seg_row, FREE),
            d_local,
            d_near,
            w_qkv,
            (hot, FREE),
            (hot_rows, FREE),
            (modulation, FREE),
            tokens,
            (d_middle, FREE),
        ],
        [shaped((length, model), F32), shaped((hot_rows.shape[0], 2 * model), F32)],
        "back_remote",
        52,
        raw=[p for pair in pairs for p in pair[:2]] + list(saved),
        scratch=back_scratch(length, width)
        + [
            pltpu.VMEM((2, 4 * width, model), LOW),
            pltpu.VMEM((2, length, 3 * width), LOW),
            pltpu.VMEM((length, 3 * width), LOW),
            pltpu.VMEM((length, model), F32),
            pltpu.SemaphoreType.DMA((2, PIECES)),
            pltpu.SemaphoreType.DMA((2,)),
        ],
    )


def mod_gradient(me, attn_sums, arrived, rest, conds):
    parts, high, model = arrived.shape
    extra = 4 * conds
    share = high - 2 * extra
    wide = rest.shape[1]

    def body(scalars, staged, raw, scratch):
        came, output = raw
        held, tails, sems = scratch
        packed = staged.outs[0]
        below = pltpu.make_async_copy(came.at[:, share:, :], tails, sems.at[parts])
        below.start()
        copies = [
            pltpu.make_async_copy(
                came.at[k, :share, :], output.at[k * share : (k + 1) * share, :], sems.at[k]
            )
            for k in range(parts)
        ]
        for c in copies:
            c.start()
        low = staged.get(0)
        held[:, : low.shape[1]] = low[:conds]
        packed[...] = staged.get(1)[...]
        below.wait()
        total = jnp.zeros((extra, model), F32)
        for k in range(parts):
            total = total + (
                tails[k, :extra].astype(F32) + tails[k, extra : 2 * extra].astype(F32)
            )
        for n in range(4):
            held[:, (2 + n) * model : (3 + n) * model] = total[n * conds : (n + 1) * conds]
        for k in range(held.shape[1] // wide):

            @pl.when(scalars[0][0] == k)
            def _():
                packed[:conds] = held[:, k * wide : (k + 1) * wide].astype(LOW).astype(F32)

        for c in copies:
            c.wait()

    return staged_call(
        body,
        [me],
        [attn_sums, (rest, FREE)],
        [shaped(rest.shape, F32)],
        "mod_gradient",
        24,
        raw=[arrived],
        raw_outs=[shaped((parts * share, model), LOW)],
        scratch=[
            pltpu.VMEM((conds, 6 * model), F32),
            pltpu.VMEM((parts, 2 * extra, model), LOW),
            pltpu.SemaphoreType.DMA((parts + 1,)),
        ],
    )


def mod_product(joined, w_ada_rows):
    wide, model = w_ada_rows.shape

    def body(scalars, staged, raw, scratch):
        staged.outs[0][...] = dot_nn(staged.get(0)[0, :8].astype(LOW), staged.get(1)[...])

    return staged_call(
        body, [], [(joined, FREE), w_ada_rows], [shaped((8, model), F32)], "mod_product", 24
    )[0]


def factors(place, blocks, columns, units, model, conds):
    wide = blocks[0].shape[2]

    def body(scalars, staged, raw, scratch):
        d_w_ada, d_b_ada, d_b_out, d_b_up, d_b_down = staged.outs

        def pair_up(values_in):
            while len(values_in) > 1:
                values_in = [a + b for a, b in zip(values_in[0::2], values_in[1::2])]
            return values_in[0]

        each = [
            staged.get(k).at[n] for k in range(len(blocks)) for n in range(blocks[k].shape[0])
        ]
        d_mod = [one[:conds] for one in each]
        d_b_ada[...] = jnp.sum(pair_up(d_mod), 0)
        biases = pair_up([one[2 * conds :] for one in each])
        d_b_out[...] = biases[0, :model]
        d_b_up[...] = biases[1, :units]
        d_b_down[...] = biases[2, :model]
        row = lax.broadcasted_iota(jnp.int32, (model, columns), 0)
        column = lax.broadcasted_iota(jnp.int32, (model, columns), 1)
        pick = (row == column + scalars[0][0] * columns).astype(LOW)
        cond = jnp.concatenate([one[conds : 2 * conds, :model] for one in each], 0).astype(LOW)
        mine = dot_nn(cond, pick).astype(LOW)
        d_w_ada[...] = dot_tn(mine, jnp.concatenate(d_mod, 0).astype(LOW))

    return staged_call(
        body,
        [place],
        [(one, FREE) for one in blocks],
        [
            shaped((columns, wide), F32),
            shaped((wide,), F32),
            shaped((model,), F32),
            shaped((units,), F32),
            shaped((model,), F32),
        ],
        "factors",
        32,
    )


def shards(
    tokens,
    conditioning,
    segments,
    crop_cond,
    w_ada,
    b_ada,
    w_qkv,
    w_out,
    b_out,
    w_up,
    b_up,
    w_down,
    b_down,
    d_out,
):
    length, width = tokens.shape
    cond_count = conditioning.shape[1]
    crop_count = crop_cond.shape[1]
    local_width = w_qkv.shape[2]
    parts = lax.axis_size("tensor")
    dp_count = lax.axis_size("dp")
    me = lax.axis_index("tensor")
    dp_me = lax.axis_index("dp")
    share = length // parts

    def from_ahead(value, step):
        return lax.ppermute(value, "tensor", [(s, (s - step) % parts) for s in range(parts)])

    def tensor_swap(value, distance):
        return lax.ppermute(value, "tensor", [(s, s ^ distance) for s in range(parts)])

    def dp_swap(value, distance):
        return lax.ppermute(value, "dp", [(s, s ^ distance) for s in range(dp_count)])

    steps = sorted(range(1, parts), key=lambda k: (-min(k, parts - k), k))

    def exchange(blocks):
        return lax.all_to_all(blocks, "tensor", 0, 0, tiled=True)

    levels = []
    left = dp_count
    stride = 1
    while left > 1:
        radix = 2 if (left % 4 or left == dp_count) and left % 2 == 0 else 4
        levels.append((stride, radix))
        stride *= radix
        left //= radix

    high = width // dp_count
    fast = [radix for _, radix in levels[:2]] == [2, dp_count // 2] and high % 16 == 0
    halves = (dp_count // 2, high) if fast else None
    dp_digit = dp_me % 2

    radix = dp_count // 2

    def dp_first(made, earlier=(), cut=0):
        if fast:
            keep, *send = made
            got = [dp_swap(one, 1) for one in send]
            return level_sum((dp_me // 2).reshape(1), keep, got, earlier, cut)
        return (dp_level(made[0].reshape(dp_count, high, -1), levels[0], dp_count),)

    def dp_level(current, level, remaining):
        stride, radix = level
        digit = (dp_me // stride) % radix
        view = current.reshape((remaining // radix, radix) + current.shape[1:])
        total = lax.dynamic_index_in_dim(view, digit, 1, False).astype(F32)
        for m in sorted(range(1, radix), reverse=True):
            piece = lax.dynamic_index_in_dim(view, digit ^ m, 1, False).astype(LOW)
            total = total + dp_swap(piece, m * stride).astype(F32)
        return total

    def dp_send(blocks):
        return [dp_swap(one, 2 * m) for m, one in enumerate(blocks, 1)]

    def dp_slow(blocks):
        (current,) = blocks
        for level in levels[1:]:
            current = dp_level(current, level, current.shape[0])
        return current[0]

    def dp_gather_first(value):
        stride, radix = levels[0]
        joined = value[None]
        return jnp.concatenate([joined] + [dp_swap(joined, m * stride) for m in range(1, radix)])

    def dp_gather_rest(joined):
        current = [joined]
        for stride, radix in levels[1:]:
            joined = current[0] if len(current) == 1 else jnp.concatenate(current)
            current = [joined] + [dp_swap(joined, m * stride) for m in range(1, radix)]
        return current

    def pair_sum(values_in):
        while values_in.shape[0] > 1:
            values_in = values_in[0::2] + values_in[1::2]
        return values_in[0]

    barrier = lax.optimization_barrier
    me_ref = me.reshape(1)
    cond_act, silu_back = jax.vjp(jax.nn.silu, conditioning.astype(F32))
    cond_low = cond_act.astype(LOW).reshape(cond_count, width)
    mod_part = (
        jnp.dot(cond_low, w_ada, preferred_element_type=F32) + b_ada.astype(F32)
    ).astype(LOW)
    mod_all = exchange(jnp.broadcast_to(mod_part[None], (parts,) + mod_part.shape))
    modulation = mod_all.transpose(1, 0, 2).reshape(cond_count, -1)
    modulation = jnp.pad(modulation, ((0, HOT - cond_count), (0, 0)))

    rows = 4 * local_width // PIECES
    slot = dp_me % PIECES
    qkv_rows = w_qkv.transpose(1, 2, 0).reshape(3 * local_width, width)
    out_rows = w_out.T
    start = slot * rows
    piece = jnp.where(
        start < 3 * local_width,
        lax.dynamic_slice_in_dim(
            qkv_rows, jnp.minimum(start, 3 * local_width - rows), rows, 0
        ),
        lax.dynamic_slice_in_dim(out_rows, jnp.maximum(start - 3 * local_width, 0), rows, 0),
    )
    table = slot ^ jnp.array(
        [2 * a + c for c in (0, 1) for a in range(PIECES // 2)], jnp.int32
    )
    in_order = jnp.arange(PIECES, dtype=jnp.int32)
    order = [1] + list(range(parts - 1, 1, -1))
    pairs = [
        (qkv_rows.reshape(-1, rows, width), out_rows.reshape(-1, rows, width), 0)
    ] + [None] * (parts - 1)
    arrived = from_ahead(piece, order[0])

    seg_col = segments.reshape(length, 1)
    crop_match = seg_col == jnp.arange(crop_count, dtype=jnp.int32)[None, :]
    token_cond = jnp.sum(jnp.where(crop_match, crop_cond.reshape(1, crop_count), 0), -1)
    hot = (token_cond[:, None] == jnp.arange(HOT, dtype=jnp.int32)[None, :]).astype(LOW)
    hot_rows = (token_cond[None, :] == jnp.arange(HOT, dtype=jnp.int32)[:, None]).astype(LOW)

    def per_token(index, chosen):
        return jnp.dot(
            chosen,
            modulation[:, index * width : (index + 1) * width],
            preferred_element_type=F32,
        )

    def pass_on(block):
        return [block, dp_swap(block, 2), dp_swap(block, 4)]

    def relay(passed):
        block, beside, above = passed
        cut = block.shape[0] // 2 // 16 * 16
        return passed + [dp_swap(above[:cut], 2), dp_swap(beside[cut:], 4)]

    def finish(passed):
        near = jnp.stack(passed[:3] + [jnp.concatenate(passed[3:])])
        return (near, dp_swap(near, 1))

    second_z = from_ahead(piece, order[1])
    modulation, arrived, second_z, piece = barrier((modulation, arrived, second_z, piece))
    nearest = jnp.concatenate([arrived, second_z])
    passed = pass_on(nearest)
    last_z = from_ahead(piece, order[2])
    resid_in = tokens.astype(F32)
    normed_attn, _ = normalize_rows(resid_in)
    first_in = (normed_attn * (1.0 + per_token(1, hot)) + per_token(0, hot)).astype(LOW)
    saved = [None] * parts
    attended = [None] * parts
    w_outs = [None] * parts

    def group(k, chosen_table):
        saved[k], attended[k], w_outs[k] = attend_group(
            chosen_table, first_in, seg_col, segments, pairs[k], local_width
        )

    group(0, in_order)
    attended[0], passed, grad_in = barrier((attended[0], passed, d_out))
    passed = relay(passed)
    d_mixed = (grad_in.astype(F32) * per_token(5, hot)).astype(LOW)
    d_b_down = jnp.sum(d_mixed.astype(F32), 0)
    d_hidden = jnp.dot(d_mixed, w_down, preferred_element_type=F32)
    d_hidden, last_z = barrier((d_hidden, last_z))
    last = pass_on(last_z)
    d_hidden, passed = barrier((d_hidden, passed))
    both = finish(passed)
    pairs[order[0]], pairs[order[1]] = both + (0,), both + (1,)
    group(order[0], table)
    attended[order[0]], last = barrier((attended[order[0]], last))
    last = relay(last)
    group(order[1], table)
    attended[order[1]], last = barrier((attended[order[1]], last))
    pairs[order[2]] = finish(last) + (0,)
    group(order[2], table)
    branch, middle, second_in, hidden, d_pre, d_second_parts, d_b_up = mlp_forward(
        me_ref,
        attended,
        w_outs,
        b_out.astype(F32).reshape(1, width),
        tokens,
        hot,
        modulation,
        d_hidden,
        w_up,
        b_up.astype(F32).reshape(1, -1),
    )
    second_arrived = exchange(d_second_parts)

    mlp_low, gate_sums = mlp_down(hidden, w_down, d_out, hot_rows, parts)
    digit_ref = dp_digit.reshape(1)
    mlp_made = mlp_grads(digit_ref, d_mixed, hidden, second_in, d_pre, halves)
    units = w_down.shape[1]
    mlp_blocks = dp_first(mlp_made, cut=units)
    second_arrived, mlp_blocks, mlp_low, gate_sums = barrier(
        (second_arrived, mlp_blocks, mlp_low, gate_sums)
    )
    spread, d_second, d_middle_own = turn_back(
        me_ref, second_arrived, modulation, middle, d_out, hot
    )
    d_middle = exchange(spread).reshape(length, width)

    half_type = shaped((high, units), F32)
    if fast:
        down_got = dp_send(mlp_blocks[1:radix])
        (d_w_down,) = finish_sum([(mlp_blocks[0], 0, units)], down_got, [half_type])
    else:
        d_w_down, d_w_up = finish_sum([(dp_slow(mlp_blocks), 0, 2 * units)], [], [half_type] * 2)
    b_down_row = b_down.astype(F32).reshape(1, width)
    sums_low = own_sums(
        me_ref,
        branch,
        middle,
        d_second,
        d_middle_own,
        d_out,
        b_down_row,
        hot_rows,
        gate_sums,
        cond_count,
    )
    d_middle, d_w_down, sums_low, mlp_low = barrier((d_middle, d_w_down, sums_low, mlp_low))
    mlp_arrived = exchange(mlp_low)
    d_branch, d_local, d_near, *attention_parts, d_b_out = back_first(
        digit_ref,
        d_middle,
        hot,
        modulation,
        seg_col,
        segments,
        out_rows,
        saved[0],
        first_in,
        attended[0],
        w_outs[1],
        saved[1],
        halves,
    )
    attention_blocks = dp_first(attention_parts, mlp_blocks[radix:])
    d_branch, mlp_arrived, attention_blocks = barrier((d_branch, mlp_arrived, attention_blocks))
    output_parts = output_rows(me_ref, mlp_arrived, b_down_row, middle, modulation, hot, sums_low)
    output_arrived = exchange(output_parts)
    d_branch, output_parts, attention_blocks = barrier((d_branch, output_parts, attention_blocks))
    rest_got = dp_send(attention_blocks[1:]) if fast else [dp_slow(attention_blocks)]
    d_tokens, attn_sums = back_remote(
        me_ref,
        table,
        d_branch,
        seg_col,
        segments,
        d_local,
        d_near,
        qkv_rows,
        hot,
        hot_rows,
        modulation,
        tokens,
        d_middle,
        pairs[1:],
        saved[1:],
    )
    attention_types = [shaped((3, high, local_width), F32), shaped((high, local_width), F32)]
    if fast:
        d_w_up, d_w_qkv, d_w_out = finish_sum(
            [(mlp_blocks[0], units, units), (attention_blocks[0], 0, 4 * local_width)],
            rest_got,
            [half_type, *attention_types],
        )
    else:
        d_w_qkv, d_w_out = finish_sum(
            [(rest_got[0], 0, 4 * local_width)], [], attention_types
        )
    d_w_qkv = d_w_qkv.transpose(1, 0, 2)
    if fast:
        attn_sums, output_arrived, d_w_qkv, d_w_out, d_w_up = barrier(
            (attn_sums, output_arrived, d_w_qkv, d_w_out, d_w_up)
        )
    mod_width = w_ada.shape[1]

    def row(values_in):
        flat = values_in.reshape(-1, values_in.shape[-1]).astype(F32)
        return jnp.pad(flat, ((0, 0), (0, mod_width - flat.shape[1])))

    others = jnp.concatenate(
        [jnp.zeros((cond_count, mod_width), F32)]
        + [row(one) for one in (cond_low, d_b_out, d_b_up, d_b_down[None])]
        + [jnp.zeros((5, mod_width), F32)]
    )
    packed, output = mod_gradient(me_ref, attn_sums, output_arrived, others, cond_count)
    joined = dp_gather_first(packed)
    gathered = dp_gather_rest(joined)
    d_silu_part = mod_product(joined, w_ada.T)
    gathered, d_silu_part = barrier((gathered, d_silu_part))
    d_silu = pair_sum(
        jnp.stack([d_silu_part] + [tensor_swap(d_silu_part, m) for m in range(1, parts)])
    )[:cond_count]
    d_conditioning = silu_back(d_silu.reshape(conditioning.shape))[0]
    d_w_ada, d_b_ada, d_b_out, d_b_up, d_b_down = factors(
        dp_me.reshape(1), gathered, width // dp_count, d_b_up.shape[1], width, cond_count
    )
    return (
        output,
        d_tokens,
        d_conditioning,
        d_w_ada,
        d_b_ada,
        d_w_qkv,
        d_w_out,
        d_b_out,
        d_w_up,
        d_b_up,
        d_w_down,
        d_b_down,
    )


def solution(mesh):
    return jax.shard_map(
        shards,
        mesh=mesh,
        in_specs=(
            P("dp", None),
            P("dp", None, None),
            P("dp", None),
            P("dp", None),
            P(None, "tensor"),
            P("tensor"),
            P(None, None, "tensor"),
            P(None, "tensor"),
            P(),
            P(None, "tensor"),
            P("tensor"),
            P(None, "tensor"),
            P(),
            P("dp", None),
        ),
        out_specs=(
            P("dp", None),
            P("dp", None),
            P("dp", None, None),
            P("dp", "tensor"),
            P("tensor"),
            P("dp", None, "tensor"),
            P("dp", "tensor"),
            P(),
            P("dp", "tensor"),
            P("tensor"),
            P("dp", "tensor"),
            P(),
        ),
        check_vma=False,
    )
```

```python
import jax
import jax.numpy as jnp
from jax import lax
from jax.experimental import pallas as pl
from jax.experimental.pallas import tpu as pltpu
from jax.sharding import PartitionSpec as P

HD = 72
F32 = jnp.float32
LOW = jnp.bfloat16
NEG = -1e30
LOG2E = 1.4426950408889634
PIECES = 8
HOT = 8
SMEM = pl.BlockSpec(memory_space=pltpu.SMEM)
HBM = pl.BlockSpec(memory_space=pltpu.HBM)
SMALL = pl.CostEstimate(flops=1 << 20, transcendentals=0, bytes_accessed=1 << 20)


def dot_nn(a, b):
    return lax.dot_general(a, b, (((1,), (0,)), ((), ())), preferred_element_type=F32)


def dot_nt(a, b):
    return lax.dot_general(a, b, (((1,), (1,)), ((), ())), preferred_element_type=F32)


def dot_tn(a, b):
    return lax.dot_general(a, b, (((0,), (0,)), ((), ())), preferred_element_type=F32)


def normalize_rows(values):
    average = jnp.mean(values, -1, keepdims=True)
    centered = values - average
    variance = jnp.mean(centered * centered, -1, keepdims=True)
    inverse = lax.rsqrt(variance + 1e-06)
    return (centered * inverse, inverse)


def normalize_back(gradient, normed, inverse):
    return inverse * (
        gradient
        - jnp.mean(gradient, -1, keepdims=True)
        - normed * jnp.mean(gradient * normed, -1, keepdims=True)
    )


def softmax_rows(queries, key_vecs, bias):
    scaled = dot_nt(queries, key_vecs) * (HD**-0.5 * LOG2E) + bias
    exponent = jnp.exp2(scaled - jnp.max(scaled, -1, keepdims=True))
    return exponent * (1.0 / jnp.sum(exponent, -1, keepdims=True))


def piece_copies(table, pair, into, sems):
    first, second, step, rows = pair
    ahead = first.shape[0]
    copies = []
    for n in range(PIECES):
        source = first.at[n] if n < ahead else second.at[n - ahead]
        source = source.at[step * rows : (step + 1) * rows, :]
        place = pl.ds(pl.multiple_of(table[n] * rows, 16), rows)
        copies.append(pltpu.make_async_copy(source, into.at[place, :], sems.at[n]))
    return copies


class Staged:
    def __init__(self, sources, ins, in_sems, outs, targets, out_sems):
        self.coming = [
            pltpu.make_async_copy(a, b, in_sems.at[n])
            for n, (a, b) in enumerate(zip(sources, ins))
        ]
        self.going = [[] for _ in outs]
        self.ins, self.outs = ins, outs
        self.here = set()
        self.pairs, self.out_sems = list(zip(outs, targets)), out_sems
        for one in self.coming:
            one.start()

    def get(self, n):
        if n not in self.here:
            self.here.add(n)
            self.coming[n].wait()
        return self.ins[n]

    def put(self, n):
        one = pltpu.make_async_copy(*self.pairs[n], self.out_sems.at[n])
        one.start()
        self.going[n].append(one)

    def put_part(self, n, part, parts, size):
        source, target = self.pairs[n]
        place = slice(part * size, (part + 1) * size)
        one = pltpu.make_async_copy(
            source.at[place], target.at[place], self.out_sems.at[len(self.pairs) * (1 + part) + n]
        )
        one.start()
        self.going[n].append(one)

    def finish(self):
        for n in range(len(self.coming)):
            self.get(n)
        for n, made in enumerate(self.going):
            if not made:
                self.put(n)
        for made in self.going:
            for one in made:
                one.wait()


OWN_ROWS = "rows"
OWN_FREE = "rows anywhere"
FREE = "anywhere"
OWN_COLUMNS = "columns"


def staged_call(
    body, scalars, ins, outs, name, mib, raw=(), raw_outs=(), scratch=(), small=True, share=0
):
    plain = [one if isinstance(one, tuple) else (one, None) for one in ins]
    arrays = [
        one if kind in (FREE, OWN_FREE) else pltpu.with_memory_space_constraint(one, pltpu.HBM)
        for one, kind in plain
    ]
    shapes = []
    for one, kind in plain:
        shape = list(one.shape)
        if kind in (OWN_ROWS, OWN_FREE):
            shape[0] = share
        if kind == OWN_COLUMNS:
            shape[1] = share
        shapes.append(pltpu.VMEM(tuple(shape), one.dtype))
    counts = [
        len(scalars),
        len(ins),
        len(raw),
        len(outs),
        len(raw_outs),
        len(ins),
        len(outs),
    ]

    def kernel(*refs):
        groups, at = [], 0
        for count in counts:
            groups.append(refs[at : at + count])
            at += count
        scalar_refs, sources, raw_refs, targets, raw_targets, in_refs, out_refs = groups
        in_sems, out_sems = refs[at : at + 2]
        picked = []
        for source, (_, kind) in zip(sources, plain):
            if kind in (OWN_ROWS, OWN_FREE):
                source = source.at[pl.ds(pl.multiple_of(scalar_refs[0][0] * share, 16), share), :]
            if kind == OWN_COLUMNS:
                source = source.at[:, pl.ds(pl.multiple_of(scalar_refs[0][0] * share, 128), share)]
            picked.append(source)
        staged = Staged(picked, in_refs, in_sems, out_refs, targets, out_sems)
        body(scalar_refs, staged, raw_refs + raw_targets, refs[at + 2 :])
        staged.finish()

    return pl.pallas_call(
        kernel,
        out_shape=tuple(pltpu.HBM(one.shape, one.dtype) for one in (*outs, *raw_outs)),
        in_specs=[SMEM] * len(scalars) + [HBM] * (len(ins) + len(raw)),
        out_specs=(HBM,) * (len(outs) + len(raw_outs)),
        scratch_shapes=shapes
        + [pltpu.VMEM(one.shape, one.dtype) for one in outs]
        + [pltpu.SemaphoreType.DMA((len(ins),)), pltpu.SemaphoreType.DMA((3 * max(len(outs), 1),))]
        + list(scratch),
        compiler_params=pltpu.CompilerParams(vmem_limit_bytes=mib << 20),
        cost_estimate=SMALL if small else None,
        name=name,
    )(*scalars, *arrays, *raw)


def shaped(shape, dtype):
    return jax.ShapeDtypeStruct(shape, dtype)


def modulate(hot, modulation, index):
    model = modulation.shape[1] // 6
    return dot_nn(hot[...], modulation[:, index * model : (index + 1) * model])


def fill_bias(bias, seg_col, seg_row):
    bias[...] = jnp.where(seg_col[...] == seg_row[...], 0.0, NEG)


def attend_group(table, first_in, seg_col, seg_row, pair, width):
    length, model = first_in.shape
    total = 4 * width

    def body(scalars, staged, raw, scratch):
        weights, bias, sems = scratch
        pieces = piece_copies(scalars[0], (*raw, pair[2], total // PIECES), weights, sems)
        for c in pieces:
            c.start()
        fill_bias(bias, staged.get(1), staged.get(2))
        projected, attended, w_out = staged.outs
        for c in pieces:
            c.wait()
        projected[...] = dot_nt(staged.get(0)[...], weights[: 3 * width]).astype(LOW)
        staged.put(0)
        w_out[...] = weights[3 * width :]
        staged.put(2)
        for h in range(width // HD):
            queries, key_vecs, values = [
                projected[:, j * width + h * HD : j * width + (h + 1) * HD] for j in range(3)
            ]
            probs = softmax_rows(queries, key_vecs, bias[...])
            attended[:, h * HD : (h + 1) * HD] = dot_nn(probs.astype(LOW), values).astype(LOW)

    return staged_call(
        body,
        [table],
        [(first_in, FREE), (seg_col, FREE), (seg_row, FREE)],
        [
            shaped((length, 3 * width), LOW),
            shaped((length, width), LOW),
            shaped((width, model), LOW),
        ],
        "attend_group",
        32,
        raw=pair[:2],
        scratch=[
            pltpu.VMEM((total, model), LOW),
            pltpu.VMEM((length, length), F32),
            pltpu.SemaphoreType.DMA((PIECES,)),
        ],
    )


def head_gradients(qkv, d_attended, bias, low_probs, d_scores, d_projected):
    width = d_attended.shape[1]
    scale = HD**-0.5
    for h in range(width // HD):
        columns = slice(h * HD, (h + 1) * HD)
        queries, key_vecs, values = [
            qkv[:, j * width + h * HD : j * width + (h + 1) * HD] for j in range(3)
        ]
        d_head = d_attended[:, columns]
        probs = softmax_rows(queries, key_vecs, bias[...])
        d_probs = dot_nt(d_head, values)
        inner = jnp.sum(d_probs * probs, -1, keepdims=True)
        low_probs[h] = probs.astype(LOW)
        d_scores[h] = (probs * (d_probs - inner)).astype(LOW)
        d_projected[:, h * HD : (h + 1) * HD] = (dot_nn(d_scores[h], key_vecs) * scale).astype(
            LOW
        )
        d_projected[:, width + h * HD : width + (h + 1) * HD] = (
            dot_tn(d_scores[h], queries) * scale
        ).astype(LOW)
        d_projected[:, 2 * width + h * HD : 2 * width + (h + 1) * HD] = dot_tn(
            low_probs[h], d_head
        ).astype(LOW)


def split_sum(hot_rows, values_in):
    high = values_in.astype(LOW)
    rest = values_in - high.astype(F32)
    mid = rest.astype(LOW)
    low = (rest - mid.astype(F32)).astype(LOW)
    return dot_nn(hot_rows, high) + dot_nn(hot_rows, mid) + dot_nn(hot_rows, low)


def mlp_forward(me, attended, w_out, b_out, tokens, hot, modulation, d_hidden, w_up, b_up):
    parts = len(attended)
    length, model = tokens.shape
    units = w_up.shape[1]
    share = length // parts

    def body(scalars, staged, raw, scratch):
        held = scratch[0]
        own_branch, own_middle, second_in, hidden, d_pre, d_second, d_b_up = staged.outs
        rows = length // 2
        sums = jnp.zeros((1, units), F32)
        for step in range(2):
            block = slice(step * rows, (step + 1) * rows)
            branch = staged.get(2 * parts)[...]
            for k in range(parts):
                branch = branch + dot_nn(staged.get(k)[block], staged.get(parts + k)[...])
            chosen, table = staged.get(2 * parts + 2)[block], staged.get(2 * parts + 3)
            stream = staged.get(2 * parts + 1)[block].astype(F32) + (
                modulate(chosen, table, 2) * branch
            )
            held[0, block] = branch
            held[1, block] = stream
            normed, _ = normalize_rows(stream)
            second = (normed * (1.0 + modulate(chosen, table, 4)) + modulate(chosen, table, 3)).astype(LOW)
            second_in[block] = second
            staged.put_part(2, step, 2, rows)
            weights = staged.get(2 * parts + 5)
            u = dot_nn(second, weights[...]) + staged.get(2 * parts + 6)[...]
            root = 0.7978845608028654
            square = u * u
            bent = jnp.tanh(root * u * (1.0 + 0.044715 * square))
            half = 0.5 * (1.0 + bent)
            hidden[block] = (u * half).astype(LOW)
            staged.put_part(3, step, 2, rows)
            slope = half + 0.5 * u * (1.0 - bent * bent) * (root * (1.0 + 3 * 0.044715 * square))
            low = (staged.get(2 * parts + 4)[block] * slope).astype(LOW)
            d_pre[block] = low
            staged.put_part(4, step, 2, rows)
            sums = sums + jnp.sum(low.astype(F32), 0, keepdims=True)
            added = dot_nt(low, weights[...]).astype(LOW)
            for n in range(rows // share):
                d_second[step * (rows // share) + n] = added[n * share : (n + 1) * share]
            staged.put_part(5, step, 2, rows // share)
        d_b_up[...] = sums
        mine = pl.ds(pl.multiple_of(scalars[0][0] * share, 8), share)
        own_branch[...] = held[0, mine, :]
        own_middle[...] = held[1, mine, :]

    return staged_call(
        body,
        [me],
        [*attended, *w_out, (b_out, FREE), tokens, (hot, FREE), (modulation, FREE), (d_hidden, FREE), w_up, (b_up, FREE)],
        [
            shaped((share, model), F32),
            shaped((share, model), F32),
            shaped((length, model), LOW),
            shaped((length, units), LOW),
            shaped((length, units), LOW),
            shaped((parts, share, model), LOW),
            shaped((1, units), F32),
        ],
        "mlp_forward",
        48,
        scratch=[pltpu.VMEM((2, length, model), F32)],
        small=False,
    )


def mlp_down(hidden, w_down, d_out, hot_rows, parts):
    length, model = d_out.shape
    share = length // parts
    count = hot_rows.shape[0]

    def body(scalars, staged, raw, scratch):
        low, sums = staged.outs
        total = jnp.zeros((count, model), F32)
        rows = length // 2
        for step in range(2):
            block = slice(step * rows, (step + 1) * rows)
            added = dot_nt(staged.get(0)[block], staged.get(1)[...])
            for n in range(rows // share):
                low[step * (rows // share) + n] = added[n * share : (n + 1) * share].astype(LOW)
            staged.put_part(0, step, 2, rows // share)
            total = total + split_sum(
                staged.get(3)[:, block], staged.get(2)[block].astype(F32) * added
            )
        sums[...] = total

    return staged_call(
        body,
        [],
        [hidden, w_down, d_out, (hot_rows, FREE)],
        [shaped((parts, share, model), LOW), shaped((count, model), F32)],
        "mlp_down",
        32,
    )


def hand_out_types(halves, rows, columns):
    if halves is None:
        return [shaped((rows, columns), F32)]
    count, high = halves
    return [shaped((count, high, columns), F32)] + [shaped((high, columns), LOW)] * count


def hand_out(digit, whole, outs):
    if len(outs) == 1:
        outs[0][...] = whole[...]
        return
    keep, *send = outs
    high = keep.shape[1]
    for n, one in enumerate(send):
        keep[n] = whole[pl.ds(pl.multiple_of((2 * n + digit) * high, 8), high), :]
        one[...] = whole[pl.ds(pl.multiple_of((2 * n + 1 - digit) * high, 8), high), :].astype(LOW)


def mlp_grads(digit, d_mixed, hidden, second_in, d_pre, halves):
    model, units = d_mixed.shape[1], hidden.shape[1]

    def body(scalars, staged, raw, scratch):
        whole = scratch[0]
        whole[:, :units] = dot_tn(staged.get(0)[...], staged.get(1)[...])
        whole[:, units:] = dot_tn(staged.get(2)[...], staged.get(3)[...])
        hand_out(scalars[0][0], whole, staged.outs)

    return staged_call(
        body,
        [digit],
        [(d_mixed, FREE), hidden, second_in, d_pre],
        hand_out_types(halves, model, 2 * units),
        "mlp_grads",
        48,
        scratch=[pltpu.VMEM((model, 2 * units), F32)],
    )


def level_sum(digit, keep, got, earlier=(), cut=0):
    radix, rows, columns = keep.shape
    before = earlier[0].shape[1] if earlier else 0
    widths = [cut, columns - cut] if cut else [before + columns]

    def body(scalars, staged, raw, scratch):
        came = scratch[0]
        mine = scalars[0][0]
        for n in range(radix):
            came[n] = staged.get(1 + n)[...]
        kept = staged.get(0)
        for m in range(1, radix):
            other = jnp.bitwise_xor(mine, m)
            total = (kept[other] + came[other].astype(F32)).astype(LOW)
            if cut:
                staged.outs[m][...] = total[:, :cut]
                staged.outs[radix - 1 + m][...] = total[:, cut:]
                staged.put(radix - 1 + m)
            else:
                if earlier:
                    staged.outs[m][:, :before] = staged.get(radix + m)[...]
                staged.outs[m][:, before:] = total
            staged.put(m)
        staged.outs[0][...] = kept[mine] + came[mine].astype(F32)

    return staged_call(
        body,
        [digit],
        [keep, *[(one, FREE) for one in got], *earlier],
        [shaped((rows, columns), F32)]
        + [shaped((rows, wide), LOW) for wide in widths for _ in range(radix - 1)],
        "level_sum",
        40,
        scratch=[pltpu.VMEM(keep.shape, LOW)],
    )


def finish_sum(owns, got, types):
    def body(scalars, staged, raw, scratch):
        n, at, base, total = 0, 0, 0, None
        for out in staged.outs:
            width = out.shape[-1]
            for j in range(out.shape[0] if len(out.shape) == 3 else 1):
                if total is None:
                    _, begin, wide = owns[n]
                    total = staged.get(n)[:, begin : begin + wide]
                    for k in range(len(got)):
                        total = total + staged.get(len(owns) + k)[:, base : base + wide].astype(F32)
                target = out.at[j] if len(out.shape) == 3 else out
                target[...] = total[:, at : at + width]
                at += width
                if at == wide:
                    n, at, base, total = n + 1, 0, base + wide, None

    return staged_call(
        body, [], [*[one[0] for one in owns], *[(one, FREE) for one in got]], types, "finish_sum", 32
    )


def turn_back(me, arrived, modulation, middle, d_out, hot):
    parts, share, model = arrived.shape

    def body(scalars, staged, raw, scratch):
        spread, d_second, d_middle = staged.outs
        normed, inverse = normalize_rows(staged.get(2)[...])
        scale = modulate(staged.get(4), staged.get(1), 4)
        came = staged.get(0)
        grad = came[0].astype(F32)
        for k in range(1, parts):
            grad = grad + came[k].astype(F32)
        d_second[...] = grad
        moved = staged.get(3)[...].astype(F32) + normalize_back(
            grad * (1.0 + scale), normed, inverse
        )
        d_middle[...] = moved
        for k in range(parts):
            spread[k] = moved.astype(LOW)

    return staged_call(
        body,
        [me],
        [(arrived, FREE), (modulation, FREE), middle, (d_out, OWN_ROWS), (hot, OWN_FREE)],
        [
            shaped(arrived.shape, LOW),
            shaped((share, model), F32),
            shaped((share, model), F32),
        ],
        "turn_back",
        16,
        share=share,
    )


def own_sums(me, branch, middle, d_second, d_middle, d_out, b_down, hot_rows, gate_sums, conds):
    share, model = middle.shape
    extra = 4 * conds

    def body(scalars, staged, raw, scratch):
        held = scratch[0]
        normed, _ = normalize_rows(staged.get(1)[...])
        second, moved = staged.get(2), staged.get(3)
        each = [
            moved[...] * staged.get(0)[...],
            second[...],
            second[...] * normed,
            staged.get(4)[...].astype(F32) * staged.get(5)[...],
        ]
        for n, one in enumerate(each):
            added = split_sum(staged.get(6)[...], one)
            if n == len(each) - 1:
                added = added + staged.get(7)[...]
            held[n * conds : (n + 1) * conds] = added[:conds]
        high = held[...].astype(LOW)
        staged.outs[0][:extra] = high
        staged.outs[0][extra:] = (held[...] - high.astype(F32)).astype(LOW)

    return staged_call(
        body,
        [me],
        [
            branch,
            middle,
            d_second,
            d_middle,
            (d_out, OWN_ROWS),
            (b_down, FREE),
            (hot_rows, OWN_COLUMNS),
            (gate_sums, FREE),
        ],
        [shaped((2 * extra, model), LOW)],
        "own_sums",
        24,
        scratch=[pltpu.VMEM((extra, model), F32)],
        share=share,
    )[0]


def output_rows(me, arrived, b_down, middle, modulation, hot, sums):
    parts, share, model = arrived.shape
    below = sums.shape[0]

    def body(scalars, staged, raw, scratch):
        came = staged.get(0)
        total = staged.get(1)[...]
        for k in range(parts):
            total = total + came[k].astype(F32)
        made = staged.get(2)[...] + modulate(staged.get(4), staged.get(3), 5) * total
        low = made.astype(LOW)
        spread = staged.outs[0]
        for k in range(parts):
            spread[k, :share] = low
            spread[k, share:] = staged.get(5)[...]

    return staged_call(
        body,
        [me],
        [
            (arrived, FREE),
            (b_down, FREE),
            middle,
            (modulation, FREE),
            (hot, OWN_FREE),
            sums,
        ],
        [shaped((parts, share + below, model), LOW)],
        "output_rows",
        24,
        share=share,
    )[0]


def back_scratch(length, width):
    heads = width // HD
    return [
        pltpu.VMEM((length, width), LOW),
        pltpu.VMEM((heads, length, length), LOW),
        pltpu.VMEM((heads, length, length), LOW),
        pltpu.VMEM((length, length), F32),
    ]


def back_first(
    digit,
    d_middle,
    hot,
    modulation,
    seg_col,
    seg_row,
    w_out,
    qkv,
    first_in,
    attended,
    near_out,
    near_qkv,
    halves,
):
    length, model = d_middle.shape
    width = attended.shape[1]

    def body(scalars, staged, raw, scratch):
        (
            d_attended,
            low_probs,
            d_scores,
            bias,
            weights,
            projected,
            d_projected,
            whole,
            sems,
        ) = scratch
        fetches = [
            pltpu.make_async_copy(raw[n], weights.at[n, 3 * width :, :], sems.at[n])
            for n in range(2)
        ] + [pltpu.make_async_copy(raw[2 + n], projected.at[n], sems.at[2 + n]) for n in range(2)]
        for c in fetches:
            c.start()
        d_branch, d_local, d_near, *outs, d_b_out = staged.outs
        gate = modulate(staged.get(1), staged.get(2), 2)
        d_branch[...] = (staged.get(0)[...].astype(F32) * gate).astype(LOW)
        staged.put(0)
        d_b_out[...] = jnp.sum(d_branch[...].astype(F32), 0, keepdims=True)
        fill_bias(bias, staged.get(3), staged.get(4))
        for c in fetches:
            c.wait()

        def group_step(group, carry):
            slot = lax.rem(group, 2)
            used = weights.at[slot]
            d_attended[...] = dot_nt(d_branch[...], used[3 * width :]).astype(LOW)
            head_gradients(
                projected.at[slot], d_attended, bias, low_probs, d_scores, d_projected
            )

            @pl.when(group == 0)
            def _():
                d_local[...] = d_projected[...]

            @pl.when(group == 1)
            def _():
                d_near[...] = d_projected[...]

            return carry

        lax.fori_loop(0, 2, group_step, 0)
        staged.put(1)
        staged.put(2)
        whole[:, : 3 * width] = dot_tn(staged.get(5)[...], d_local[...])
        whole[:, 3 * width :] = dot_tn(d_branch[...], staged.get(6)[...])
        hand_out(scalars[0][0], whole, outs)

    return staged_call(
        body,
        [digit],
        [
            (d_middle, FREE),
            (hot, FREE),
            (modulation, FREE),
            (seg_col, FREE),
            (seg_row, FREE),
            (first_in, FREE),
            attended,
        ],
        [
            shaped((length, model), LOW),
            shaped((length, 3 * width), LOW),
            shaped((length, 3 * width), LOW),
            *hand_out_types(halves, model, 4 * width),
            shaped((1, model), F32),
        ],
        "back_first",
        52,
        raw=[w_out, near_out, qkv, near_qkv],
        scratch=back_scratch(length, width)
        + [
            pltpu.VMEM((2, 4 * width, model), LOW),
            pltpu.VMEM((2, length, 3 * width), LOW),
            pltpu.VMEM((length, 3 * width), LOW),
            pltpu.VMEM((model, 4 * width), F32),
            pltpu.SemaphoreType.DMA((4,)),
        ],
    )


def back_remote(
    me,
    table,
    d_branch,
    seg_col,
    seg_row,
    d_local,
    d_near,
    w_qkv,
    hot,
    hot_rows,
    modulation,
    tokens,
    d_middle,
    pairs,
    saved,
):
    length, model = d_branch.shape
    width = d_local.shape[1] // 3
    remote = len(saved)
    parts = remote + 1
    rows = 4 * width // PIECES

    def body(scalars, staged, raw, scratch):
        (
            d_attended,
            low_probs,
            d_scores,
            bias,
            weights,
            projected,
            d_projected,
            d_first,
            sems,
            saved_sems,
        ) = scratch
        me_ref, table_ref = scalars
        pieces, qkvs = raw[: 2 * remote], raw[2 * remote :]
        d_tokens, sums = staged.outs

        def copies(k, slot):
            pair = (pieces[2 * k - 2], pieces[2 * k - 1], pairs[k - 1][2], rows)
            return piece_copies(table_ref, pair, weights.at[slot], sems.at[slot]) + [
                pltpu.make_async_copy(qkvs[k - 1], projected.at[slot], saved_sems.at[slot])
            ]

        def ahead_of(group):
            return lax.rem(group - me_ref[0] + parts, parts)

        def fetch(group, slot):
            for k in range(1, parts):

                @pl.when(ahead_of(group) == k)
                def _():
                    for c in copies(k, slot):
                        c.start()

        fetch(0, 0)
        d_first[...] = jnp.zeros_like(d_first)
        fill_bias(bias, staged.get(1), staged.get(2))
        branch_grad, own_grad, near_grad, own_weights = [staged.get(n) for n in (0, 3, 4, 5)]

        def group_step(group, carry):
            slot = lax.rem(group, 2)

            @pl.when(group < parts - 1)
            def _():
                fetch(group + 1, 1 - slot)

            used = weights.at[slot]

            @pl.when(ahead_of(group) == 0)
            def _():
                d_projected[...] = own_grad[...]
                used[: 3 * width] = own_weights[...]

            @pl.when(ahead_of(group) != 0)
            def _():
                for c in copies(1, slot):
                    c.wait()

            @pl.when(ahead_of(group) == 1)
            def _():
                d_projected[...] = near_grad[...]

            @pl.when(ahead_of(group) > 1)
            def _():
                d_attended[...] = dot_nt(branch_grad[...], used[3 * width :]).astype(LOW)
                head_gradients(
                    projected.at[slot], d_attended, bias, low_probs, d_scores, d_projected
                )

            d_first[...] += dot_nn(d_projected[...], used[: 3 * width])
            return carry

        lax.fori_loop(0, parts, group_step, 0)
        total = jnp.zeros(sums.shape, F32)
        step = length // 4
        chosen, turned, modulation_ref, tokens_ref, middle_ref = [
            staged.get(n) for n in (6, 7, 8, 9, 10)
        ]
        for r in range(4):
            block = slice(r * step, (r + 1) * step)
            normed, inverse = normalize_rows(tokens_ref[block].astype(F32))
            scale = modulate(chosen[block], modulation_ref, 1)
            grad = d_first[block]
            d_tokens[block] = middle_ref[block].astype(F32) + normalize_back(
                grad * (1.0 + scale), normed, inverse
            )
            total = total + jnp.concatenate(
                [split_sum(turned[:, block], v) for v in (grad, grad * normed)], 1
            )
        sums[...] = total

    return staged_call(
        body,
        [me, table],
        [
            d_branch,
            (seg_col, FREE),
            (seg_row, FREE),
            d_local,
            d_near,
            w_qkv,
            (hot, FREE),
            (hot_rows, FREE),
            (modulation, FREE),
            tokens,
            (d_middle, FREE),
        ],
        [shaped((length, model), F32), shaped((hot_rows.shape[0], 2 * model), F32)],
        "back_remote",
        52,
        raw=[p for pair in pairs for p in pair[:2]] + list(saved),
        scratch=back_scratch(length, width)
        + [
            pltpu.VMEM((2, 4 * width, model), LOW),
            pltpu.VMEM((2, length, 3 * width), LOW),
            pltpu.VMEM((length, 3 * width), LOW),
            pltpu.VMEM((length, model), F32),
            pltpu.SemaphoreType.DMA((2, PIECES)),
            pltpu.SemaphoreType.DMA((2,)),
        ],
    )


def mod_gradient(me, attn_sums, arrived, rest, conds):
    parts, high, model = arrived.shape
    extra = 4 * conds
    share = high - 2 * extra
    wide = rest.shape[1]

    def body(scalars, staged, raw, scratch):
        came, output = raw
        held, tails, packed, sems = scratch
        below = pltpu.make_async_copy(came.at[:, share:, :], tails, sems.at[parts])
        below.start()
        copies = [
            pltpu.make_async_copy(
                came.at[k, :share, :], output.at[k * share : (k + 1) * share, :], sems.at[k]
            )
            for k in range(parts)
        ]
        for c in copies:
            c.start()
        low = staged.get(0)
        held[:, : low.shape[1]] = low[:conds]
        packed[...] = staged.get(1)[...]
        below.wait()
        total = jnp.zeros((extra, model), F32)
        for k in range(parts):
            total = total + (
                tails[k, :extra].astype(F32) + tails[k, extra : 2 * extra].astype(F32)
            )
        for n in range(4):
            held[:, (2 + n) * model : (3 + n) * model] = total[n * conds : (n + 1) * conds]
        for k in range(held.shape[1] // wide):

            @pl.when(scalars[0][0] == k)
            def _():
                packed[:conds] = held[:, k * wide : (k + 1) * wide].astype(LOW).astype(F32)

        staged.outs[0][...] = packed[...].astype(LOW)
        staged.put(0)
        for c in copies:
            c.wait()

    return staged_call(
        body,
        [me],
        [attn_sums, (rest, FREE)],
        [shaped(rest.shape, LOW)],
        "mod_gradient",
        24,
        raw=[arrived],
        raw_outs=[shaped((parts * share, model), LOW)],
        scratch=[
            pltpu.VMEM((conds, 6 * model), F32),
            pltpu.VMEM((parts, 2 * extra, model), LOW),
            pltpu.VMEM(rest.shape, F32),
            pltpu.SemaphoreType.DMA((parts + 1,)),
        ],
    )


def mod_product(joined, w_ada_rows):
    wide, model = w_ada_rows.shape

    def body(scalars, staged, raw, scratch):
        staged.outs[0][...] = dot_nn(staged.get(0)[0], staged.get(1)[...])[:8]

    return staged_call(
        body, [], [(joined, FREE), w_ada_rows], [shaped((8, model), F32)], "mod_product", 24
    )[0]


def factors(place, blocks, columns, units, model, conds):
    wide = blocks[0].shape[2]

    def body(scalars, staged, raw, scratch):
        d_w_ada, d_b_ada, d_b_out, d_b_up, d_b_down = staged.outs

        def pair_up(values_in):
            while len(values_in) > 1:
                values_in = [a + b for a, b in zip(values_in[0::2], values_in[1::2])]
            return values_in[0]

        each = [
            staged.get(k)[n].astype(F32)
            for k in range(len(blocks))
            for n in range(blocks[k].shape[0])
        ]
        d_mod = [one[:conds] for one in each]
        d_b_ada[...] = jnp.sum(pair_up(d_mod), 0)
        biases = pair_up(
            [one[2 * conds : 2 * conds + 3] + one[2 * conds + 3 : 2 * conds + 6] for one in each]
        )
        d_b_out[...] = biases[0, :model]
        d_b_up[...] = biases[1, :units]
        d_b_down[...] = biases[2, :model]
        row = lax.broadcasted_iota(jnp.int32, (model, columns), 0)
        column = lax.broadcasted_iota(jnp.int32, (model, columns), 1)
        pick = (row == column + scalars[0][0] * columns).astype(LOW)
        cond = jnp.concatenate([one[conds : 2 * conds, :model] for one in each], 0).astype(LOW)
        mine = dot_nn(cond, pick).astype(LOW)
        d_w_ada[...] = dot_tn(mine, jnp.concatenate(d_mod, 0).astype(LOW))

    return staged_call(
        body,
        [place],
        [(one, FREE) for one in blocks],
        [
            shaped((columns, wide), F32),
            shaped((wide,), F32),
            shaped((model,), F32),
            shaped((units,), F32),
            shaped((model,), F32),
        ],
        "factors",
        32,
    )


def shards(
    tokens,
    conditioning,
    segments,
    crop_cond,
    w_ada,
    b_ada,
    w_qkv,
    w_out,
    b_out,
    w_up,
    b_up,
    w_down,
    b_down,
    d_out,
):
    length, width = tokens.shape
    cond_count = conditioning.shape[1]
    crop_count = crop_cond.shape[1]
    local_width = w_qkv.shape[2]
    parts = lax.axis_size("tensor")
    dp_count = lax.axis_size("dp")
    me = lax.axis_index("tensor")
    dp_me = lax.axis_index("dp")
    share = length // parts

    def from_ahead(value, step):
        return lax.ppermute(value, "tensor", [(s, (s - step) % parts) for s in range(parts)])

    def tensor_swap(value, distance):
        return lax.ppermute(value, "tensor", [(s, s ^ distance) for s in range(parts)])

    def dp_swap(value, distance):
        return lax.ppermute(value, "dp", [(s, s ^ distance) for s in range(dp_count)])

    steps = sorted(range(1, parts), key=lambda k: (-min(k, parts - k), k))

    def exchange(blocks):
        return lax.all_to_all(blocks, "tensor", 0, 0, tiled=True)

    levels = []
    left = dp_count
    stride = 1
    while left > 1:
        radix = 2 if (left % 4 or left == dp_count) and left % 2 == 0 else 4
        levels.append((stride, radix))
        stride *= radix
        left //= radix

    high = width // dp_count
    fast = [radix for _, radix in levels[:2]] == [2, dp_count // 2] and high % 16 == 0
    halves = (dp_count // 2, high) if fast else None
    dp_digit = dp_me % 2

    radix = dp_count // 2

    def dp_first(made, earlier=(), cut=0):
        if fast:
            keep, *send = made
            got = [dp_swap(one, 1) for one in send]
            return level_sum((dp_me // 2).reshape(1), keep, got, earlier, cut)
        return (dp_level(made[0].reshape(dp_count, high, -1), levels[0], dp_count),)

    def dp_level(current, level, remaining):
        stride, radix = level
        digit = (dp_me // stride) % radix
        view = current.reshape((remaining // radix, radix) + current.shape[1:])
        total = lax.dynamic_index_in_dim(view, digit, 1, False).astype(F32)
        for m in sorted(range(1, radix), reverse=True):
            piece = lax.dynamic_index_in_dim(view, digit ^ m, 1, False).astype(LOW)
            total = total + dp_swap(piece, m * stride).astype(F32)
        return total

    def dp_send(blocks):
        return [dp_swap(one, 2 * m) for m, one in enumerate(blocks, 1)]

    def dp_slow(blocks):
        (current,) = blocks
        for level in levels[1:]:
            current = dp_level(current, level, current.shape[0])
        return current[0]

    def dp_gather_first(value):
        stride, radix = levels[0]
        joined = value[None]
        return jnp.concatenate([joined] + [dp_swap(joined, m * stride) for m in range(1, radix)])

    def dp_gather_rest(joined):
        current = [joined]
        for stride, radix in levels[1:]:
            joined = current[0] if len(current) == 1 else jnp.concatenate(current)
            current = [joined] + [dp_swap(joined, m * stride) for m in range(1, radix)]
        return current

    def pair_sum(values_in):
        while values_in.shape[0] > 1:
            values_in = values_in[0::2] + values_in[1::2]
        return values_in[0]

    barrier = lax.optimization_barrier
    me_ref = me.reshape(1)
    cond_act, silu_back = jax.vjp(jax.nn.silu, conditioning.astype(F32))
    cond_low = cond_act.astype(LOW).reshape(cond_count, width)
    mod_part = (
        jnp.dot(cond_low, w_ada, preferred_element_type=F32) + b_ada.astype(F32)
    ).astype(LOW)
    mod_all = exchange(jnp.broadcast_to(mod_part[None], (parts,) + mod_part.shape))
    modulation = mod_all.transpose(1, 0, 2).reshape(cond_count, -1)
    modulation = jnp.pad(modulation, ((0, HOT - cond_count), (0, 0)))

    rows = 4 * local_width // PIECES
    slot = dp_me % PIECES
    qkv_rows = w_qkv.transpose(1, 2, 0).reshape(3 * local_width, width)
    out_rows = w_out.T
    start = slot * rows
    piece = jnp.where(
        start < 3 * local_width,
        lax.dynamic_slice_in_dim(
            qkv_rows, jnp.minimum(start, 3 * local_width - rows), rows, 0
        ),
        lax.dynamic_slice_in_dim(out_rows, jnp.maximum(start - 3 * local_width, 0), rows, 0),
    )
    table = slot ^ jnp.array(
        [2 * a + c for c in (0, 1) for a in range(PIECES // 2)], jnp.int32
    )
    in_order = jnp.arange(PIECES, dtype=jnp.int32)
    order = [1] + list(range(parts - 1, 1, -1))
    pairs = [
        (qkv_rows.reshape(-1, rows, width), out_rows.reshape(-1, rows, width), 0)
    ] + [None] * (parts - 1)
    arrived = from_ahead(piece, order[0])

    seg_col = segments.reshape(length, 1)
    crop_match = seg_col == jnp.arange(crop_count, dtype=jnp.int32)[None, :]
    token_cond = jnp.sum(jnp.where(crop_match, crop_cond.reshape(1, crop_count), 0), -1)
    hot = (token_cond[:, None] == jnp.arange(HOT, dtype=jnp.int32)[None, :]).astype(LOW)
    hot_rows = (token_cond[None, :] == jnp.arange(HOT, dtype=jnp.int32)[:, None]).astype(LOW)

    def per_token(index, chosen):
        return jnp.dot(
            chosen,
            modulation[:, index * width : (index + 1) * width],
            preferred_element_type=F32,
        )

    def pass_on(block):
        return [block, dp_swap(block, 2), dp_swap(block, 4)]

    def relay(passed):
        block, beside, above = passed
        cut = block.shape[0] // 2 // 16 * 16
        return passed + [dp_swap(above[:cut], 2), dp_swap(beside[cut:], 4)]

    def finish(passed):
        near = jnp.stack(passed[:3] + [jnp.concatenate(passed[3:])])
        return (near, dp_swap(near, 1))

    second_z = from_ahead(piece, order[1])
    modulation, arrived, second_z, piece = barrier((modulation, arrived, second_z, piece))
    nearest = jnp.concatenate([arrived, second_z])
    passed = pass_on(nearest)
    last_z = from_ahead(piece, order[2])
    resid_in = tokens.astype(F32)
    normed_attn, _ = normalize_rows(resid_in)
    first_in = (normed_attn * (1.0 + per_token(1, hot)) + per_token(0, hot)).astype(LOW)
    saved = [None] * parts
    attended = [None] * parts
    w_outs = [None] * parts

    def group(k, chosen_table):
        saved[k], attended[k], w_outs[k] = attend_group(
            chosen_table, first_in, seg_col, segments, pairs[k], local_width
        )

    group(0, in_order)
    attended[0], passed, grad_in = barrier((attended[0], passed, d_out))
    passed = relay(passed)
    d_mixed = (grad_in.astype(F32) * per_token(5, hot)).astype(LOW)
    d_b_down = jnp.sum(d_mixed.astype(F32), 0)
    d_hidden = jnp.dot(d_mixed, w_down, preferred_element_type=F32)
    d_hidden, last_z = barrier((d_hidden, last_z))
    last = pass_on(last_z)
    d_hidden, passed = barrier((d_hidden, passed))
    both = finish(passed)
    pairs[order[0]], pairs[order[1]] = both + (0,), both + (1,)
    group(order[0], table)
    attended[order[0]], last = barrier((attended[order[0]], last))
    last = relay(last)
    group(order[1], table)
    attended[order[1]], last = barrier((attended[order[1]], last))
    pairs[order[2]] = finish(last) + (0,)
    group(order[2], table)
    branch, middle, second_in, hidden, d_pre, d_second_parts, d_b_up = mlp_forward(
        me_ref,
        attended,
        w_outs,
        b_out.astype(F32).reshape(1, width),
        tokens,
        hot,
        modulation,
        d_hidden,
        w_up,
        b_up.astype(F32).reshape(1, -1),
    )
    second_arrived = exchange(d_second_parts)

    mlp_low, gate_sums = mlp_down(hidden, w_down, d_out, hot_rows, parts)
    digit_ref = dp_digit.reshape(1)
    mlp_made = mlp_grads(digit_ref, d_mixed, hidden, second_in, d_pre, halves)
    units = w_down.shape[1]
    mlp_blocks = dp_first(mlp_made, cut=units)
    second_arrived, mlp_blocks, mlp_low, gate_sums = barrier(
        (second_arrived, mlp_blocks, mlp_low, gate_sums)
    )
    spread, d_second, d_middle_own = turn_back(
        me_ref, second_arrived, modulation, middle, d_out, hot
    )
    d_middle = exchange(spread).reshape(length, width)

    half_type = shaped((high, units), F32)
    if fast:
        down_got = dp_send(mlp_blocks[1:radix])
        (d_w_down,) = finish_sum([(mlp_blocks[0], 0, units)], down_got, [half_type])
    else:
        d_w_down, d_w_up = finish_sum([(dp_slow(mlp_blocks), 0, 2 * units)], [], [half_type] * 2)
    b_down_row = b_down.astype(F32).reshape(1, width)
    sums_low = own_sums(
        me_ref,
        branch,
        middle,
        d_second,
        d_middle_own,
        d_out,
        b_down_row,
        hot_rows,
        gate_sums,
        cond_count,
    )
    d_middle, d_w_down, sums_low, mlp_low = barrier((d_middle, d_w_down, sums_low, mlp_low))
    mlp_arrived = exchange(mlp_low)
    d_branch, d_local, d_near, *attention_parts, d_b_out = back_first(
        digit_ref,
        d_middle,
        hot,
        modulation,
        seg_col,
        segments,
        out_rows,
        saved[0],
        first_in,
        attended[0],
        w_outs[1],
        saved[1],
        halves,
    )
    attention_blocks = dp_first(attention_parts, mlp_blocks[radix:])
    d_branch, mlp_arrived, attention_blocks = barrier((d_branch, mlp_arrived, attention_blocks))
    output_parts = output_rows(me_ref, mlp_arrived, b_down_row, middle, modulation, hot, sums_low)
    output_arrived = exchange(output_parts)
    d_branch, output_parts, attention_blocks = barrier((d_branch, output_parts, attention_blocks))
    rest_got = dp_send(attention_blocks[1:]) if fast else [dp_slow(attention_blocks)]
    d_tokens, attn_sums = back_remote(
        me_ref,
        table,
        d_branch,
        seg_col,
        segments,
        d_local,
        d_near,
        qkv_rows,
        hot,
        hot_rows,
        modulation,
        tokens,
        d_middle,
        pairs[1:],
        saved[1:],
    )
    attention_types = [shaped((3, high, local_width), F32), shaped((high, local_width), F32)]
    if fast:
        d_w_up, d_w_qkv, d_w_out = finish_sum(
            [(mlp_blocks[0], units, units), (attention_blocks[0], 0, 4 * local_width)],
            rest_got,
            [half_type, *attention_types],
        )
    else:
        d_w_qkv, d_w_out = finish_sum(
            [(rest_got[0], 0, 4 * local_width)], [], attention_types
        )
    d_w_qkv = d_w_qkv.transpose(1, 0, 2)
    if fast:
        attn_sums, output_arrived, d_w_qkv, d_w_out, d_w_up = barrier(
            (attn_sums, output_arrived, d_w_qkv, d_w_out, d_w_up)
        )
    mod_width = w_ada.shape[1]

    def row(values_in):
        flat = values_in.reshape(-1, values_in.shape[-1]).astype(F32)
        return jnp.pad(flat, ((0, 0), (0, mod_width - flat.shape[1])))

    biases = jnp.concatenate([row(one) for one in (d_b_out, d_b_up, d_b_down[None])])
    high_terms = lax.reduce_precision(biases, 8, 7)
    others = jnp.concatenate(
        [
            jnp.zeros((cond_count, mod_width), F32),
            row(cond_low),
            high_terms,
            biases - high_terms,
            jnp.zeros((2, mod_width), F32),
        ]
    )
    packed, output = mod_gradient(me_ref, attn_sums, output_arrived, others, cond_count)
    joined = dp_gather_first(packed)
    gathered = dp_gather_rest(joined)
    d_silu_part = mod_product(joined, w_ada.T)
    gathered, d_silu_part = barrier((gathered, d_silu_part))
    d_silu = pair_sum(
        jnp.stack([d_silu_part] + [tensor_swap(d_silu_part, m) for m in range(1, parts)])
    )[:cond_count]
    d_conditioning = silu_back(d_silu.reshape(conditioning.shape))[0]
    d_w_ada, d_b_ada, d_b_out, d_b_up, d_b_down = factors(
        dp_me.reshape(1), gathered, width // dp_count, d_b_up.shape[1], width, cond_count
    )
    return (
        output,
        d_tokens,
        d_conditioning,
        d_w_ada,
        d_b_ada,
        d_w_qkv,
        d_w_out,
        d_b_out,
        d_w_up,
        d_b_up,
        d_w_down,
        d_b_down,
    )


def solution(mesh):
    return jax.shard_map(
        shards,
        mesh=mesh,
        in_specs=(
            P("dp", None),
            P("dp", None, None),
            P("dp", None),
            P("dp", None),
            P(None, "tensor"),
            P("tensor"),
            P(None, None, "tensor"),
            P(None, "tensor"),
            P(),
            P(None, "tensor"),
            P("tensor"),
            P(None, "tensor"),
            P(),
            P("dp", None),
        ),
        out_specs=(
            P("dp", None),
            P("dp", None),
            P("dp", None, None),
            P("dp", "tensor"),
            P("tensor"),
            P("dp", None, "tensor"),
            P("dp", "tensor"),
            P(),
            P("dp", "tensor"),
            P("tensor"),
            P("dp", "tensor"),
            P(),
        ),
        check_vma=False,
    )
```
